256 devices in a mesh: grp: 8 (over x, core), row: 32 (over y, z).
Axes of the slice: x: 4, y: 4, z: 8, core: 2. Of those that a mesh axis runs over, the one named last changes fastest.
Arguments:
- matrix: float32 [524288, 512], P(('grp', 'row')), may hold values from -1 to 1
- targets: float32 [524288, 128], P(('grp', 'row')), may hold values from -8 to 8
- sign_bits: int32 [524288], P(('grp', 'row')), may hold values from 0 to 1
- picked_rows: int32 [256, 1024], P(('grp', 'row')), may hold values from 0 to 2047, as said below
Outputs:
- factor: float32 [512, 512], replicated
- solution: float32 [512, 128], replicated
- residual: float32 [524288, 128], P(('grp', 'row'))
The draws below stay inside these ranges and needn't reach their ends.
Inputs may be any that keep to these rules, and one draw needn't show every extreme that they name: Each row of picked_rows holds 1024 different numbers.
All inputs are finite; a program needn't handle non-finite values.
Results may differ from the reference program's by a relative error of at most 0.0003.
Values sent between devices are 32-bit elements; how exact they have to be, the bound alone decides.
No kernel may reach another device: no remote copies, remote signals or barrier semaphores. Data moves between devices by JAX's collectives and lax.ppermute only.
A program may use at most 64 MiB of HBM per device.

```python
import math
import jax
import jax.numpy as jnp
from jax import lax

N = 512
NRHS = 128
SK = 1024
ROWS_DEV = 2048
ITERS = 2
BLOCKS = 256
ROWS = 524288


def make_system(key):
    subkeys = jax.random.split(key, 5)
    row_scale = jnp.exp(jax.random.uniform(subkeys[0], (ROWS, 1)) * math.log(10.0))
    entries = jnp.clip(jax.random.normal(subkeys[2], (ROWS, N)), -5.0, 5.0)
    noise_part = 0.5 * jax.random.normal(subkeys[4], (ROWS, NRHS))
    col_scale = jnp.exp(jax.random.uniform(subkeys[1], (1, N)) * math.log(10.0))
    matrix = jnp.clip(entries * row_scale * col_scale / (10.0 * math.sqrt(N)), -1.0, 1.0)
    truth_weights = jax.random.normal(subkeys[3], (N, NRHS))
    targets = jnp.clip(jnp.dot(matrix, truth_weights) + noise_part, -8.0, 8.0)
    return (matrix.astype(jnp.float32), targets.astype(jnp.float32))


def draw_matrix(key, part):
    return make_system(jax.random.fold_in(key, 11))[0]


def draw_targets(key, part):
    return make_system(jax.random.fold_in(key, 11))[1]


def draw_picked_rows(key, part):
    subkeys = jax.random.split(jax.random.fold_in(key, 23), BLOCKS)

    def pick_rows(subkey):
        return jax.random.permutation(subkey, ROWS_DEV)[:SK]
    return jax.vmap(pick_rows)(subkeys).astype(jnp.int32)


def with_ends(values, stream_key, least, largest):
    place = [jax.random.randint(jax.random.fold_in(stream_key, axis), (), 0, length) for axis, length in enumerate(values.shape)]
    longest = values.shape.index(max(values.shape))
    next_to = place[:longest] + [(place[longest] + 1) % values.shape[longest]] + place[longest + 1:]
    return values.at[tuple(place)].set(least).at[tuple(next_to)].set(largest)


def setup_inputs(seed: int = 0) -> dict:
    arg_keys = jax.random.split(jax.random.key(seed), 5)
    matrix = draw_matrix(jax.random.fold_in(arg_keys[4], 71), 0)
    targets = draw_targets(jax.random.fold_in(arg_keys[4], 71), 0)
    sign_bits = with_ends(jax.random.randint(arg_keys[2], (ROWS,), 0, 2), jax.random.fold_in(arg_keys[2], 1), 0, 1).astype(jnp.int32)
    picked_rows = draw_picked_rows(jax.random.fold_in(arg_keys[4], 71), 0)
    return dict(matrix=matrix, targets=targets, sign_bits=sign_bits, picked_rows=picked_rows)


def walsh_transform(row_block):
    row_count, unknowns = row_block.shape
    stride = 1
    result = row_block
    while stride < row_count:
        paired = result.reshape(row_count // (2 * stride), 2, stride, unknowns)
        first_half = paired[:, 0]
        second_half = paired[:, 1]
        result = jnp.stack([first_half + second_half, first_half - second_half], axis=1).reshape(row_count, unknowns)
        stride = stride * 2
    return result

def solve_with(factor, rhs_matrix):
    inner = lax.linalg.triangular_solve(factor, rhs_matrix, left_side=True, lower=True)
    return lax.linalg.triangular_solve(factor, inner, left_side=True, lower=True, transpose_a=True)

def reference(matrix, targets, sign_bits, picked_rows):
    sign_flips = (1 - 2 * sign_bits).astype(jnp.float32)
    blocks = (matrix * sign_flips[:, None]).reshape(BLOCKS, ROWS_DEV, N)

    def add_block(running, packed):
        row_block, chosen = packed
        transformed = walsh_transform(row_block)
        return (running + jnp.take(transformed, chosen, axis=0), None)
    sketch, unused = lax.scan(add_block, jnp.zeros((SK, N), jnp.float32), (blocks, picked_rows))
    gram_scale = N / (SK * ROWS)
    gram = gram_scale * jnp.dot(sketch.T.astype(jnp.float32), sketch.astype(jnp.float32), precision=lax.Precision.HIGHEST, preferred_element_type=jnp.float32)
    factor = jnp.linalg.cholesky(gram)
    grad_scale = N / ROWS
    solution = jnp.zeros((N, NRHS), jnp.float32)
    current = targets
    for sweep in range(ITERS):
        gradient = grad_scale * jnp.dot(matrix.T.astype(jnp.float32), current.astype(jnp.float32), precision=lax.Precision.HIGHEST, preferred_element_type=jnp.float32)
        solution = solution + solve_with(factor, gradient)
        current = targets - jnp.dot(matrix.astype(jnp.float32), solution.astype(jnp.float32), precision=lax.Precision.HIGHEST, preferred_element_type=jnp.float32)
    return (factor, solution, current)
```

```python
import jax
import jax.numpy as jnp
from jax import lax
from jax.experimental import pallas as pl
from jax.experimental.pallas import tpu as pltpu
from jax.sharding import PartitionSpec as P


N = 512
NRHS = 128
SK = 1024
ROWS_DEV = 2048
ITERS = 2
NB = 128
WIDE = N + NRHS
HI = lax.Precision.HIGHEST
F32 = jnp.float32
BF16 = jnp.bfloat16
V = pltpu.VMEM
SIZES = {"core": 2, "x": 4, "y": 4, "z": 8}
NN = (((1,), (0,)), ((), ()))
TN = (((0,), (0,)), ((), ()))


def coord(name):
    g, r = lax.axis_index("grp"), lax.axis_index("row")
    return {"core": g % 2, "x": g // 2, "y": r // 8, "z": r % 8}[name]


def ahead(name, s):
    return lax.rem(coord(name) + s, SIZES[name])


def behind(name, s):
    return lax.rem(coord(name) + SIZES[name] - s, SIZES[name])


def shifted(v, name, s):
    if name == "core":
        return lax.ppermute(v, "grp", [(i, i ^ 1) for i in range(8)])
    if name == "x":
        return lax.ppermute(v, "grp", [(i, (i + 2 * s) % 8) for i in range(8)])
    if name == "y":
        return lax.ppermute(v, "row", [(i, (i + 8 * s) % 32) for i in range(32)])
    return lax.ppermute(v, "row", [(i, i // 8 * 8 + (i + s) % 8) for i in range(32)])


def scattered(chunks, name):
    return [chunks[0]] + [shifted(chunks[s], name, s) for s in range(1, SIZES[name])]


def spread(own, name):
    return [own] + [shifted(own, name, s) for s in range(1, SIZES[name])]


def shape(*dims):
    return jax.ShapeDtypeStruct(dims, F32)


def call(body, outs, ins, name, scratch=(), cost=None):
    return pl.pallas_call(
        body,
        out_shape=outs,
        in_specs=[pl.BlockSpec(memory_space=V)] * len(ins),
        out_specs=[pl.BlockSpec(memory_space=V)] * len(outs),
        scratch_shapes=list(scratch),
        name=name,
        cost_estimate=cost,
    )(*ins)


def total(refs):
    vals = [r[...] for r in refs]
    while len(vals) > 1:
        half = len(vals) // 2
        vals = [vals[i] + vals[i + half] for i in range(half)]
    return vals[0]


def split(v):
    hi = v.astype(BF16)
    return hi, (v - hi.astype(F32)).astype(BF16)


def dot(a, b, dims=NN):
    return lax.dot_general(a, b, dims, preferred_element_type=F32)


def dot_hi(a, b, dims=NN):
    return lax.dot_general(a, b, dims, precision=HI, preferred_element_type=F32)


def parity(v, bits):
    shift = 8
    while shift:
        if shift < bits:
            v = v ^ (v >> shift)
        shift //= 2
    return v & 1


def sketch_body(a_ref, sign_ref, pick_ref, keep_ref, send_ref, base_ref, high_ref, acc_ref):
    k = pl.program_id(0)
    depth = a_ref.shape[0]

    @pl.when(k == 0)
    def _():
        lane = lax.broadcasted_iota(jnp.int32, (NB, depth), 1)
        for b in range(SK // NB):
            row = pick_ref[0:1, b * NB : (b + 1) * NB]
            col = jnp.broadcast_to(row, (NB, NB)).T
            both = jnp.concatenate([col] * (depth // NB), axis=1)
            low = both & (depth - 1)
            base_ref[b * NB : (b + 1) * NB, :] = (1 - 2 * parity(low & lane, 8)).astype(F32).astype(BF16)
            high_ref[b * NB : (b + 1) * NB, :] = col >> 8
        acc_ref[...] = jnp.zeros_like(acc_ref)

    flips = (1 - 2 * sign_ref[pl.ds(k, 1), :]).astype(F32)
    hi, lo = split(a_ref[...])
    for b in range(SK // NB):
        rows = slice(b * NB, (b + 1) * NB)
        turn = (1 - 2 * parity(high_ref[rows, :] & k, 4)).astype(F32)
        turn = jnp.concatenate([turn] * (depth // NB), axis=1) * flips
        h = base_ref[rows, :] * turn.astype(BF16)
        acc_ref[rows, :] += dot(h, hi) + dot(h, lo)

    @pl.when(k == pl.num_programs(0) - 1)
    def _():
        half = SK // 2
        keep_ref[...] = acc_ref[pl.ds(pl.multiple_of(ahead("core", 0) * half, half), half), :]
        send_ref[...] = acc_ref[pl.ds(pl.multiple_of(ahead("core", 1) * half, half), half), :]


def sketch_rows(matrix, sign_bits, picked_rows):
    depth = 256
    whole = lambda k: (0, 0)
    return pl.pallas_call(
        sketch_body,
        out_shape=[shape(SK // 2, N)] * 2,
        grid=(ROWS_DEV // depth,),
        in_specs=[
            pl.BlockSpec((depth, N), lambda k: (k, 0)),
            pl.BlockSpec((ROWS_DEV // depth, depth), whole),
            pl.BlockSpec((1, SK), whole),
        ],
        out_specs=[pl.BlockSpec((SK // 2, N), whole)] * 2,
        scratch_shapes=[V((SK, depth), BF16), V((SK, NB), jnp.int32), V((SK, N), F32)],
        name="sketch",
        cost_estimate=pl.CostEstimate(flops=2 * 2 * SK * ROWS_DEV * N, bytes_accessed=8 << 20, transcendentals=0),
    )(matrix, sign_bits.reshape(ROWS_DEV // depth, depth), picked_rows)


def normal_body(a_ref, t_ref, after_ref, keep_ref, send_ref, acc_ref):
    k = pl.program_id(0)

    @pl.when(k == 0)
    def _():
        acc_ref[...] = jnp.zeros_like(acc_ref)

    hi, lo = split(a_ref[...])
    thi, tlo = split(t_ref[...])
    his, los = jnp.concatenate([hi, thi], axis=1), jnp.concatenate([lo, tlo], axis=1)
    acc_ref[...] += dot(hi, his, TN) + dot(hi, los, TN) + dot(lo, his, TN)

    @pl.when(k == pl.num_programs(0) - 1)
    def _():
        half = N // 2
        keep_ref[...] = acc_ref[pl.ds(pl.multiple_of(ahead("core", 0) * half, half), half), :]
        send_ref[...] = acc_ref[pl.ds(pl.multiple_of(ahead("core", 1) * half, half), half), :]


def normal_parts(matrix, targets, after):
    depth = 256
    whole = lambda k: (0, 0)
    return pl.pallas_call(
        normal_body,
        out_shape=[shape(N // 2, WIDE)] * 2,
        grid=(ROWS_DEV // depth,),
        in_specs=[
            pl.BlockSpec((depth, N), lambda k: (k, 0)),
            pl.BlockSpec((depth, NRHS), lambda k: (k, 0)),
            pl.BlockSpec((8, NB), whole),
        ],
        out_specs=[pl.BlockSpec((N // 2, WIDE), whole)] * 2,
        scratch_shapes=[V((N, WIDE), F32)],
        name="normal",
        cost_estimate=pl.CostEstimate(flops=3 * 2 * ROWS_DEV * N * WIDE, bytes_accessed=8 << 20, transcendentals=0),
    )(matrix, targets, after)


def after_core(own, got):
    def body(own_ref, got_ref, *outs):
        a, b, buf = outs[:4], outs[4:8], outs[8]
        buf[...] = (own_ref[...] + got_ref[...]).reshape(4, 4, 32, N)
        for s in range(4):
            a[s][...] = buf[pl.ds(ahead("x", s), 1), :, :, : N // 2][0]
            b[s][...] = buf[:, pl.ds(ahead("y", s), 1), :, N // 2 :][:, 0]

    outs = call(body, [shape(4, 32, N // 2)] * 8, [own, got], "after_core", [V((4, 4, 32, N), F32)])
    return outs[:4], outs[4:]


def after_first(a, b):
    def body(*refs):
        ins, outs, buf = refs[:8], refs[8:16], refs[16]
        for h, (first, name) in enumerate(((0, "y"), (4, "x"))):
            buf[h] = total(ins[first : first + 4])
            for s in range(4):
                outs[first + s][...] = buf[h, pl.ds(ahead(name, s), 1)][0]

    outs = call(body, [shape(32, N // 2)] * 8, [*a, *b], "after_first", [V((2, 4, 32, N // 2), F32)])
    return outs[:4], outs[4:]


def after_second(a, b):
    def body(*refs):
        ins, outs, buf = refs[:8], refs[8:16], refs[16]
        buf[...] = jnp.concatenate([total(ins[:4]), total(ins[4:])], axis=1).reshape(8, 4, N)
        for s in range(8):
            outs[s][...] = buf[pl.ds(ahead("z", s), 1)][0]

    return call(body, [shape(4, N)] * 8, [*a, *b], "after_second", [V((8, 4, N), F32)])


def summed(parts, name):
    def body(*refs):
        refs[-1][...] = total(refs[:-1])

    return call(body, [shape(*parts[0].shape)], parts, name)[0]


def after_z(parts):
    def body(*refs):
        ins, (a, b), buf = refs[:8], refs[8:10], refs[10]
        for s in range(8):
            buf[pl.ds(behind("z", s), 1)] = ins[s][...][None]
        rows = buf[...].reshape(32, N)
        a[...] = rows[:, : N // 2]
        b[...] = rows[:, N // 2 :]

    return call(body, [shape(32, N // 2)] * 2, parts, "after_z", [V((8, 4, N), F32)])


def after_back(a, b):
    def body(*refs):
        for first, name, out in ((0, "y", refs[8]), (4, "x", refs[9])):
            for s in range(4):
                out[pl.ds(behind(name, s), 1)] = refs[first + s][...][None]

    return call(body, [shape(4, 32, N // 2)] * 2, [*a, *b], "after_back")


def gram(a, b):
    def body(*refs):
        ins, out, buf = refs[:8], refs[8], refs[9]
        for s in range(4):
            buf[pl.ds(behind("x", s), 1), :, :, : N // 2] = ins[s][...][None]
            buf[:, pl.ds(behind("y", s), 1), :, N // 2 :] = ins[4 + s][...][:, None]
        rows = buf[...].reshape(SK // 2, N)
        hi, lo = split(rows)
        cross = dot(hi, lo, TN)
        out[...] = dot(hi, hi, TN) + (cross + cross.T)

    return call(body, [shape(N, N)], [*a, *b], "gram", [V((4, 4, 32, N), F32)])[0]


def to_chunks(parts, name, label):
    n = SIZES[name]
    rows = parts[0].shape[0] // n

    def body(*refs):
        ins, outs, buf = refs[: len(parts)], refs[len(parts) : -1], refs[-1]
        buf[...] = total(ins).reshape(buf.shape)
        for s in range(n):
            outs[s][...] = buf[pl.ds(ahead(name, s), 1)][0]

    return call(body, [shape(rows, WIDE)] * n, parts, label, [V((n, rows, WIDE), F32)])


def to_whole(parts, name, label):
    n = SIZES[name]
    rows = parts[0].shape[0]

    def body(*refs):
        ins, out, buf = refs[:n], refs[n], refs[n + 1]
        for s in range(n):
            buf[pl.ds(behind(name, s), 1)] = ins[s][...][None]
        out[...] = buf[...].reshape(out.shape)

    return call(body, [shape(n * rows, WIDE)], parts, label, [V((n, rows, WIDE), F32)])[0]


def normal_sums(keep, got):
    parts = scattered(to_chunks([keep, got], "z", "n_core"), "z")
    parts = scattered(to_chunks(parts, "x", "n_z"), "x")
    parts = spread(summed(parts, "n_x"), "y")
    part = summed(parts, "n_y")
    part = to_whole(spread(part, "x"), "x", "n_back_x")
    part = to_whole(spread(part, "z"), "z", "n_back_z")
    return part, shifted(part, "core", 1)


def rows_of(v, k):
    return jnp.broadcast_to(v[k : k + 1, :], (8, v.shape[1]))


def lanes_of(v, j):
    return jnp.broadcast_to(v[:, j : j + 1], (8, NB))


def factor_block(d_ref, b_ref, u_ref, w_ref):
    lane = lax.broadcasted_iota(jnp.int32, (8, NB), 1)
    sub = lax.broadcasted_iota(jnp.int32, (8, NB), 0)

    def packed(vs):
        v = vs[0]
        for m in range(1, 8):
            v = jnp.where(sub == m, vs[m], v)
        return v

    for p in range(NB // 8):
        q = 8 * p
        cols = [lanes_of(d_ref[q : q + 8, :], q + m) for m in range(8)]
        s = {(k, m): rows_of(cols[m], k) for m in range(8) for k in range(m, 8)}
        l, r = {}, {}
        for m in range(8):
            r[m] = lax.rsqrt(s[m, m])
            for k in range(m + 1, 8):
                l[k, m] = s[k, m] * r[m]
            for k in range(m + 1, 8):
                for j in range(m + 1, k + 1):
                    s[k, j] = s[k, j] - l[k, m] * l[j, m]

        def forward(vs):
            out = []
            for m in range(8):
                v = vs[m]
                for k in range(m):
                    v = v - l[m, k] * out[k]
                out.append(v * r[m])
            return out

        t, tb = d_ref[q : q + 8, :], b_ref[q : q + 8, :]
        u = forward([rows_of(t, m) for m in range(8)])
        w = forward([rows_of(tb, m) for m in range(8)])
        u_ref[q : q + 8, :] = jnp.where(lane >= q + sub, packed(u), 0.0)
        w_ref[q : q + 8, :] = packed(w)
        for i in range(p + 1, NB // 8):
            o = 8 * i
            v, y = d_ref[o : o + 8, :], b_ref[o : o + 8, :]
            c = forward([lanes_of(v, q + m) for m in range(8)])
            for m in range(8):
                v = v - c[m] * u[m]
                y = y - c[m] * w[m]
            d_ref[o : o + 8, :] = v
            b_ref[o : o + 8, :] = y


def factor_body(scale, own_ref, got_ref, l_ref, li_ref, a_ref, b_ref, d_ref, db_ref, w_ref, lt_ref):
    a_ref[...] = (own_ref[...] + got_ref[...]) * scale
    row = lax.broadcasted_iota(jnp.int32, (NB, NB), 0)
    eye = (row == lax.broadcasted_iota(jnp.int32, (NB, NB), 1)).astype(F32)
    lt_ref[...] = jnp.zeros_like(lt_ref)
    li_ref[...] = jnp.zeros_like(li_ref)
    b_ref[...] = jnp.zeros_like(b_ref)
    for j in range(N // NB):
        o, e = j * NB, (j + 1) * NB
        d_ref[...] = a_ref[o:e, o:e]
        db_ref[...] = eye
        factor_block(d_ref, db_ref, lt_ref.at[o:e, o:e], w_ref)
        w = w_ref[...]
        li_ref[o:e, o:e] = w
        if j:
            li_ref[o:e, 0:o] = dot_hi(w, b_ref[o:e, 0:o])
        if e < N:
            u = dot_hi(w, a_ref[o:e, e:])
            lt_ref[o:e, e:] = u
            a_ref[e:, e:] = a_ref[e:, e:] - dot_hi(u, u, TN)
            b_ref[e:, 0:e] = b_ref[e:, 0:e] - dot_hi(u, li_ref[o:e, 0:e], TN)
    l_ref[...] = lt_ref[...].T


def factored(own, got, scale):
    def body(*refs):
        factor_body(scale, *refs)

    scratch = [V((N, N), F32)] * 2 + [V((NB, NB), F32)] * 3 + [V((N, N), F32)]
    return call(body, [shape(N, N)] * 2, [own, got], "factor", scratch)


def solved(inverse, own, got, scale):
    def body(li_ref, own_ref, got_ref, x_ref, m_ref):
        half = N // 2
        m_ref[pl.ds(pl.multiple_of(ahead("core", 0) * half, half), half), :] = own_ref[...] * scale
        m_ref[pl.ds(pl.multiple_of(ahead("core", 1) * half, half), half), :] = got_ref[...] * scale
        first = m_ref[:, N:]
        x = jnp.zeros_like(first)
        for sweep in range(ITERS):
            gradient = first - dot_hi(m_ref[:, :N], x) if sweep else first
            x = x + dot_hi(li_ref[...], dot_hi(li_ref[...], gradient), TN)
        x_ref[...] = x

    return call(body, [shape(N, NRHS)], [inverse, own, got], "solve", [V((N, WIDE), F32)])[0]


def residual_body(a_ref, t_ref, x_ref, out_ref):
    hi, lo = split(a_ref[...])
    xhi, xlo = split(x_ref[...])
    out_ref[...] = t_ref[...] - (dot(hi, xhi) + (dot(hi, xlo) + dot(lo, xhi)))


def residual_of(matrix, targets, x):
    depth = 256
    return pl.pallas_call(
        residual_body,
        out_shape=shape(ROWS_DEV, NRHS),
        grid=(ROWS_DEV // depth,),
        in_specs=[
            pl.BlockSpec((depth, N), lambda k: (k, 0)),
            pl.BlockSpec((depth, NRHS), lambda k: (k, 0)),
            pl.BlockSpec((N, NRHS), lambda k: (0, 0)),
        ],
        out_specs=pl.BlockSpec((depth, NRHS), lambda k: (k, 0)),
        name="residual",
    )(matrix, targets, x)


def on_device(matrix, targets, sign_bits, picked_rows):
    total_rows = matrix.shape[0] * lax.axis_size("grp") * lax.axis_size("row")
    keep, send = sketch_rows(matrix, sign_bits, picked_rows)
    a, b = after_core(keep, shifted(send, "core", 1))
    nkeep, nsend = normal_parts(matrix, targets, a[0].reshape(128, 256)[:8, :NB])
    a, b = after_first(scattered(a, "x"), scattered(b, "y"))
    a, b = scattered(a, "y"), scattered(b, "x")
    nown, ngot = normal_sums(nkeep, shifted(nsend, "core", 1))
    part = summed(scattered(after_second(a, b), "z"), "after_sum")
    a, b = after_z(spread(part, "z"))
    a, b = after_back(spread(a, "y"), spread(b, "x"))
    own = gram(spread(a, "x"), spread(b, "y"))
    factor, inverse = factored(own, shifted(own, "core", 1), N / (SK * total_rows))
    x = solved(inverse, nown, ngot, N / total_rows)
    return factor, x, residual_of(matrix, targets, x)


def solution(mesh):
    rows = P(("grp", "row"), None)
    return jax.shard_map(
        on_device,
        mesh=mesh,
        in_specs=(rows, rows, P(("grp", "row")), rows),
        out_specs=(P(), P(), rows),
        check_vma=False,
    )
```

```python
import jax
import jax.numpy as jnp
from jax import lax
from jax.experimental import pallas as pl
from jax.experimental.pallas import tpu as pltpu
from jax.sharding import PartitionSpec as P

N = 512
NRHS = 128
SK = 1024
ROWS_DEV = 2048
ITERS = 2
NB = 128
UNITS = 128
TALL = 24
HI = lax.Precision.HIGHEST
F32 = jnp.float32
BF16 = jnp.bfloat16
V = pltpu.VMEM
NN = (((1,), (0,)), ((), ()))
TN = (((0,), (0,)), ((), ()))
MIB = 1 << 20
LOWER = [(i, j) for i in range(4) for j in range(i + 1)]


def core():
    return lax.rem(lax.axis_index("grp"), 2)


def shape(*dims):
    return jax.ShapeDtypeStruct(dims, F32)


def split(v):
    hi = v.astype(BF16)
    return hi, (v - hi.astype(F32)).astype(BF16)


def dot(a, b, dims=NN):
    return lax.dot_general(a, b, dims, preferred_element_type=F32)


def dot_hi(a, b, dims=NN):
    return lax.dot_general(a, b, dims, precision=HI, preferred_element_type=F32)


def parity(v, bits):
    shift = 8
    while shift:
        if shift < bits:
            v = v ^ (v >> shift)
        shift //= 2
    return v & 1


def terms_body(a_ref, t_ref, sign_ref, pick_ref, keep_ref, send_ref, base_ref, high_ref, acc_ref, nacc_ref, p_ref):
    k = pl.program_id(0)
    depth = a_ref.shape[0]

    @pl.when(k == 0)
    def _():
        lane = lax.broadcasted_iota(jnp.int32, (NB, depth), 1)
        for b in range(SK // NB):
            row = pick_ref[0:1, b * NB : (b + 1) * NB]
            col = jnp.broadcast_to(row, (NB, NB)).T
            both = jnp.concatenate([col] * (depth // NB), axis=1)
            base_ref[b * NB : (b + 1) * NB, :] = (1 - 2 * parity(both & (depth - 1) & lane, 8)).astype(F32).astype(BF16)
            high_ref[b * NB : (b + 1) * NB, :] = col >> 8
        acc_ref[...] = jnp.zeros_like(acc_ref)
        nacc_ref[...] = jnp.zeros_like(nacc_ref)

    flips = jnp.concatenate([sign_ref[pl.ds(2 * k, 1), :], sign_ref[pl.ds(2 * k + 1, 1), :]], axis=1)
    flips = (1 - 2 * flips).astype(F32)
    hi, lo = split(a_ref[...])
    for b in range(SK // NB):
        rows = slice(b * NB, (b + 1) * NB)
        turn = (1 - 2 * parity(high_ref[rows, :] & k, 4)).astype(F32)
        turn = jnp.concatenate([turn] * (depth // NB), axis=1) * flips
        h = base_ref[rows, :] * turn.astype(BF16)
        acc_ref[rows, :] += dot(h, hi) + dot(h, lo)

    thi, tlo = split(t_ref[...])
    his, los = jnp.concatenate([thi, hi], axis=1), jnp.concatenate([tlo, lo], axis=1)
    hit, lot = hi.T, lo.T
    for i in range(4):
        rows, wide = slice(i * NB, (i + 1) * NB), (i + 2) * NB
        nacc_ref[rows, :wide] += dot(hit[rows], his[:, :wide]) + (dot(hit[rows], los[:, :wide]) + dot(lot[rows], his[:, :wide]))

    @pl.when(k == pl.num_programs(0) - 1)
    def _():
        for i in range(4):
            p_ref[0, i] = nacc_ref[i * NB : (i + 1) * NB, :NB]
        for b, (i, j) in enumerate(LOWER):
            p_ref[(b + 4) // 8, (b + 4) % 8] = nacc_ref[i * NB : (i + 1) * NB, (j + 1) * NB : (j + 2) * NB]
        p_ref[1, 6:] = jnp.zeros_like(p_ref[1, 6:])
        for out, half in ((keep_ref, core()), (send_ref, 1 - core())):

            def put(r, _, out=out, half=half):
                rows = acc_ref[pl.ds(pl.multiple_of(half * (SK // 2) + r * 16, 16), 16), :]
                for c in range(4):
                    out[pl.ds(r * 4 + c, 1), :16, :] = rows[:, c * NB : (c + 1) * NB][None]
                block = p_ref[pl.ds(half, 1), pl.ds(r // 4, 1), pl.ds(pl.multiple_of(lax.rem(r, 4) * 32, 32), 32), :]
                out[pl.ds(r * 4, 4), 16:, :] = block.reshape(4, 8, NB)
                return 0

            lax.fori_loop(0, 32, put, 0)


def terms(matrix, targets, sign_bits, picked_rows):
    depth = 256
    whole = lambda k: (0, 0)
    return pl.pallas_call(
        terms_body,
        out_shape=[shape(UNITS, TALL, NB)] * 2,
        grid=(ROWS_DEV // depth,),
        in_specs=[
            pl.BlockSpec((depth, N), lambda k: (k, 0)),
            pl.BlockSpec((depth, NRHS), lambda k: (k, 0)),
            pl.BlockSpec((ROWS_DEV // NB, NB), whole),
            pl.BlockSpec((1, SK), whole),
        ],
        out_specs=[pl.BlockSpec((UNITS, TALL, NB), lambda k: (0, 0, 0))] * 2,
        scratch_shapes=[
            V((SK, depth), BF16),
            V((SK, NB), jnp.int32),
            V((SK, N), F32),
            V((N, N + NRHS), F32),
            V((2, 8, NB, NB), F32),
        ],
        compiler_params=pltpu.CompilerParams(vmem_limit_bytes=32 * MIB),
        name="terms",
    )(matrix, targets, sign_bits.reshape(ROWS_DEV // NB, NB), picked_rows)


def other_core(v):
    return lax.ppermute(v, "grp", [(i, i ^ 1) for i in range(8)])


def over_x(v):
    groups = [[0, 2, 4, 6], [1, 3, 5, 7]]
    return lax.all_to_all(v, "grp", 0, 0, axis_index_groups=groups, tiled=True)


def over_row(v):
    return lax.all_to_all(v, "row", 0, 0, tiled=True)


def summed(keep, send):
    v = (keep + other_core(send)).reshape(4, 32, TALL, NB)
    v = jnp.sum(over_x(v), axis=0)
    v = jnp.sum(over_row(v), axis=0)
    v = over_row(jnp.broadcast_to(v, (32, TALL, NB)))
    v = over_x(jnp.broadcast_to(v, (4, 32, TALL, NB)))
    return v.reshape(UNITS, TALL, NB)


def gram_body(in_ref, out_ref, s_ref):
    def take(r, _):
        for c in range(4):
            s_ref[pl.ds(pl.multiple_of(r * 16, 16), 16), c * NB : (c + 1) * NB] = in_ref[pl.ds(r * 4 + c, 1), :16, :][0]
        out_ref[pl.ds(pl.multiple_of(len(LOWER) * NB + r * 32, 32), 32), :] = in_ref[pl.ds(r * 4, 4), 16:, :].reshape(32, NB)
        return 0

    lax.fori_loop(0, 32, take, 0)
    hi, lo = split(s_ref[...])
    hit, lot = hi.T, lo.T
    for i in range(4):
        rows, wide = slice(i * NB, (i + 1) * NB), (i + 1) * NB
        g = dot(hit[rows], hi[:, :wide]) + (dot(hit[rows], lo[:, :wide]) + dot(lot[rows], hi[:, :wide]))
        for j in range(i + 1):
            b = LOWER.index((i, j))
            out_ref[b * NB : (b + 1) * NB, :] = g[:, j * NB : (j + 1) * NB]


def gram(v):
    return pl.pallas_call(
        gram_body,
        out_shape=shape((len(LOWER) + 8) * NB, NB),
        in_specs=[pl.BlockSpec(memory_space=V)],
        out_specs=pl.BlockSpec(memory_space=V),
        scratch_shapes=[V((SK // 2, N), F32)],
        compiler_params=pltpu.CompilerParams(vmem_limit_bytes=16 * MIB),
        name="gram",
    )(v)


def rows_of(v, k):
    return jnp.broadcast_to(v[k : k + 1, :], (8, v.shape[1]))


def lanes_of(v, j):
    return jnp.broadcast_to(v[:, j : j + 1], (8, NB))


def factor_block(d_ref, b_ref, u_ref, w_ref):
    lane = lax.broadcasted_iota(jnp.int32, (8, NB), 1)
    sub = lax.broadcasted_iota(jnp.int32, (8, NB), 0)

    def packed(vs):
        v = vs[0]
        for m in range(1, 8):
            v = jnp.where(sub == m, vs[m], v)
        return v

    for p in range(NB // 8):
        q = 8 * p
        cols = [lanes_of(d_ref[q : q + 8, :], q + m) for m in range(8)]
        s = {(k, m): rows_of(cols[m], k) for m in range(8) for k in range(m, 8)}
        l, r = {}, {}
        for m in range(8):
            r[m] = lax.rsqrt(s[m, m])
            for k in range(m + 1, 8):
                l[k, m] = s[k, m] * r[m]
            for k in range(m + 1, 8):
                for j in range(m + 1, k + 1):
                    s[k, j] = s[k, j] - l[k, m] * l[j, m]

        def forward(vs):
            out = []
            for m in range(8):
                v = vs[m]
                for k in range(m):
                    v = v - l[m, k] * out[k]
                out.append(v * r[m])
            return out

        t, tb = d_ref[q : q + 8, :], b_ref[q : q + 8, :]
        u = forward([rows_of(t, m) for m in range(8)])
        w = forward([rows_of(tb, m) for m in range(8)])
        u_ref[q : q + 8, :] = jnp.where(lane >= q + sub, packed(u), 0.0)
        w_ref[q : q + 8, :] = packed(w)
        for i in range(p + 1, NB // 8):
            o = 8 * i
            v, y = d_ref[o : o + 8, :], b_ref[o : o + 8, :]
            c = forward([lanes_of(v, q + m) for m in range(8)])
            for m in range(8):
                v = v - c[m] * u[m]
                y = y - c[m] * w[m]
            d_ref[o : o + 8, :] = v
            b_ref[o : o + 8, :] = y


def finish_body(
    gram_scale, grad_scale, own_ref, got_ref, a_hbm, t_hbm, l_ref, x_ref, r_hbm,
    a_ref, b_ref, d_ref, db_ref, w_ref, u_ref, lt_ref, li_ref, m_ref, mat_ref, t_ref, r_ref, sems,
):
    fetch = [pltpu.make_async_copy(a_hbm, mat_ref, sems.at[0]), pltpu.make_async_copy(t_hbm, t_ref, sems.at[1])]
    for copy in fetch:
        copy.start()
    zeros = jnp.zeros((NB, NB), F32)
    for b, (i, j) in enumerate(LOWER):
        rows = slice(b * NB, (b + 1) * NB)
        g = (own_ref[rows, :] + got_ref[rows, :]) * gram_scale
        a_ref[i * NB : (i + 1) * NB, j * NB : (j + 1) * NB] = g
        if i != j:
            a_ref[j * NB : (j + 1) * NB, i * NB : (i + 1) * NB] = g.T
    lt_ref[...] = jnp.zeros_like(lt_ref)
    li_ref[...] = jnp.zeros_like(li_ref)
    b_ref[...] = jnp.zeros_like(b_ref)
    row = lax.broadcasted_iota(jnp.int32, (NB, NB), 0)
    eye = (row == lax.broadcasted_iota(jnp.int32, (NB, NB), 1)).astype(F32)

    def block(step, _):
        here = pl.ds(pl.multiple_of(step * NB, NB), NB)
        d_ref[...] = a_ref[here, here]
        db_ref[...] = eye
        factor_block(d_ref, db_ref, u_ref, w_ref)
        lt_ref[here, here] = u_ref[...]
        li_ref[here, here] = w_ref[...]
        for j in range(N // NB):

            @pl.when(step == j)
            def _(j=j):
                o, e = j * NB, (j + 1) * NB
                w = w_ref[...]
                if j:
                    li_ref[o:e, 0:o] = dot_hi(w, b_ref[o:e, 0:o])
                if e < N:
                    u = dot_hi(w, a_ref[o:e, e:])
                    lt_ref[o:e, e:] = u
                    ut = u.T
                    a_ref[e:, e:] = a_ref[e:, e:] - dot_hi(ut, u)
                    b_ref[e:, 0:e] = b_ref[e:, 0:e] - dot_hi(ut, li_ref[o:e, 0:e])

        return 0

    lax.fori_loop(0, N // NB, block, 0)
    l_ref[...] = lt_ref[...].T

    base = len(LOWER) * NB

    def moment(b):
        at = pl.ds(base + (b % 8) * NB, NB)
        mine = own_ref[at, :]
        other = got_ref[at, :]
        return jnp.where(core() == b // 8, mine, other) * grad_scale

    first = jnp.concatenate([moment(i) for i in range(4)], axis=0)
    for b, (i, j) in enumerate(LOWER):
        g = moment(b + 4)
        m_ref[i * NB : (i + 1) * NB, j * NB : (j + 1) * NB] = g
        if i != j:
            m_ref[j * NB : (j + 1) * NB, i * NB : (i + 1) * NB] = g.T

    def times(parts, v):
        hi, lo = split(v)
        both = jnp.concatenate([hi, lo], axis=1)
        ahead, behind = dot(parts[0], both), dot(parts[1], both)
        return ahead[:, :NRHS] + ((ahead[:, NRHS:] + behind[:, :NRHS]) + behind[:, NRHS:])

    inverse, turned, moments = split(li_ref[...]), split(li_ref[...].T), split(m_ref[...])
    x = times(turned, times(inverse, first))
    for _ in range(ITERS - 1):
        x = x + times(turned, times(inverse, first - times(moments, x)))
    x_ref[...] = x
    for copy in fetch:
        copy.wait()
    xs = jnp.concatenate(split(x), axis=1)
    puts = []
    deep = ROWS_DEV // 4
    for c in range(4):
        rows = slice(c * deep, (c + 1) * deep)
        hi, lo = split(mat_ref[rows, :])
        ahead, behind = dot(hi, xs), dot(lo, xs)
        r_ref[rows, :] = t_ref[rows, :] - (ahead[:, :NRHS] + ((ahead[:, NRHS:] + behind[:, :NRHS]) + behind[:, NRHS:]))
        puts.append(pltpu.make_async_copy(r_ref.at[rows, :], r_hbm.at[rows, :], sems.at[2 + c]))
        puts[-1].start()
    for copy in puts:
        copy.wait()


def finished(own, got, matrix, targets, gram_scale, grad_scale):
    def body(*refs):
        finish_body(gram_scale, grad_scale, *refs)

    vmem, hbm = pl.BlockSpec(memory_space=V), pl.BlockSpec(memory_space=pl.ANY)
    return pl.pallas_call(
        body,
        out_shape=[shape(N, N), shape(N, NRHS), shape(ROWS_DEV, NRHS)],
        in_specs=[vmem, vmem, hbm, hbm],
        out_specs=[vmem, vmem, hbm],
        scratch_shapes=[V((N, N), F32)] * 2
        + [V((NB, NB), F32)] * 4
        + [V((N, N), F32)] * 3
        + [V((ROWS_DEV, N), F32)]
        + [V((ROWS_DEV, NRHS), F32)] * 2
        + [pltpu.SemaphoreType.DMA((6,))],
        compiler_params=pltpu.CompilerParams(vmem_limit_bytes=40 * MIB),
        name="finish",
    )(own, got, matrix, targets)


def on_device(matrix, targets, sign_bits, picked_rows):
    total_rows = matrix.shape[0] * lax.axis_size("grp") * lax.axis_size("row")
    keep, send = terms(matrix, targets, sign_bits, picked_rows)
    own = gram(summed(keep, send))
    return tuple(finished(own, other_core(own), matrix, targets, N / (SK * total_rows), N / total_rows))


def solution(mesh):
    rows = P(("grp", "row"), None)
    return jax.shard_map(
        on_device,
        mesh=mesh,
        in_specs=(rows, rows, P(("grp", "row")), rows),
        out_specs=(P(), P(), rows),
        check_vma=False,
    )
```

```python
import jax
import jax.numpy as jnp
from jax import lax
from jax.experimental import pallas as pl
from jax.experimental.pallas import tpu as pltpu
from jax.sharding import PartitionSpec as P

N = 512
NRHS = 128
SK = 1024
ROWS_DEV = 2048
ITERS = 2
NB = 128
UNITS = 128
TALL = 24
HI = lax.Precision.HIGHEST
F32 = jnp.float32
BF16 = jnp.bfloat16
V = pltpu.VMEM
NN = (((1,), (0,)), ((), ()))
TN = (((0,), (0,)), ((), ()))
MIB = 1 << 20
LOWER = [(i, j) for i in range(4) for j in range(i + 1)]


def core():
    return lax.rem(lax.axis_index("grp"), 2)


def shape(*dims):
    return jax.ShapeDtypeStruct(dims, F32)


def split(v):
    hi = v.astype(BF16)
    return hi, (v - hi.astype(F32)).astype(BF16)


def dot(a, b, dims=NN):
    return lax.dot_general(a, b, dims, preferred_element_type=F32)


def dot_hi(a, b, dims=NN):
    return lax.dot_general(a, b, dims, precision=HI, preferred_element_type=F32)


def parity(v, bits):
    shift = 8
    while shift:
        if shift < bits:
            v = v ^ (v >> shift)
        shift //= 2
    return v & 1


def terms_body(a_ref, t_ref, sign_ref, pick_ref, keep_ref, send_ref, base_ref, high_ref, acc_ref, nacc_ref, p_ref):
    k = pl.program_id(0)
    depth = a_ref.shape[0]

    @pl.when(k == 0)
    def _():
        lane = lax.broadcasted_iota(jnp.int32, (NB, depth), 1)
        for b in range(SK // NB):
            row = pick_ref[0:1, b * NB : (b + 1) * NB]
            col = jnp.broadcast_to(row, (NB, NB)).T
            both = jnp.concatenate([col] * (depth // NB), axis=1)
            base_ref[b * NB : (b + 1) * NB, :] = (1 - 2 * parity(both & (depth - 1) & lane, 8)).astype(F32).astype(BF16)
            high_ref[b * NB : (b + 1) * NB, :] = col >> 8
        acc_ref[...] = jnp.zeros_like(acc_ref)
        nacc_ref[...] = jnp.zeros_like(nacc_ref)

    flips = jnp.concatenate([sign_ref[pl.ds(2 * k, 1), :], sign_ref[pl.ds(2 * k + 1, 1), :]], axis=1)
    flips = (1 - 2 * flips).astype(F32)
    hi, lo = split(a_ref[...])
    for b in range(SK // NB):
        rows = slice(b * NB, (b + 1) * NB)
        turn = (1 - 2 * parity(high_ref[rows, :] & k, 4)).astype(F32)
        turn = jnp.concatenate([turn] * (depth // NB), axis=1) * flips
        h = base_ref[rows, :] * turn.astype(BF16)
        acc_ref[rows, :] += dot(h, hi) + dot(h, lo)

    thi, tlo = split(t_ref[...])
    his, los = jnp.concatenate([thi, hi], axis=1), jnp.concatenate([tlo, lo], axis=1)
    hit, lot = hi.T, lo.T
    for i in range(4):
        rows, wide = slice(i * NB, (i + 1) * NB), (i + 2) * NB
        nacc_ref[rows, :wide] += dot(hit[rows], his[:, :wide]) + (dot(hit[rows], los[:, :wide]) + dot(lot[rows], his[:, :wide]))

    @pl.when(k == pl.num_programs(0) - 1)
    def _():
        for i in range(4):
            p_ref[0, i] = nacc_ref[i * NB : (i + 1) * NB, :NB]
        for b, (i, j) in enumerate(LOWER):
            p_ref[(b + 4) // 8, (b + 4) % 8] = nacc_ref[i * NB : (i + 1) * NB, (j + 1) * NB : (j + 2) * NB]
        p_ref[1, 6:] = jnp.zeros_like(p_ref[1, 6:])
        for out, half in ((keep_ref, core()), (send_ref, 1 - core())):

            def put(r, _, out=out, half=half):
                rows = acc_ref[pl.ds(pl.multiple_of(half * (SK // 2) + r * 16, 16), 16), :]
                for c in range(4):
                    out[pl.ds(r * 4 + c, 1), :16, :] = rows[:, c * NB : (c + 1) * NB][None]
                block = p_ref[pl.ds(half, 1), pl.ds(r // 4, 1), pl.ds(pl.multiple_of(lax.rem(r, 4) * 32, 32), 32), :]
                out[pl.ds(r * 4, 4), 16:, :] = block.reshape(4, 8, NB)
                return 0

            lax.fori_loop(0, 32, put, 0)


def in_hbm(v):
    return pltpu.with_memory_space_constraint(v, pltpu.HBM)


def terms(matrix, targets, sign_bits, picked_rows):
    depth = 256
    whole = lambda k: (0, 0)
    return pl.pallas_call(
        terms_body,
        out_shape=[shape(UNITS, TALL, NB)] * 2,
        grid=(ROWS_DEV // depth,),
        in_specs=[
            pl.BlockSpec((depth, N), lambda k: (k, 0)),
            pl.BlockSpec((depth, NRHS), lambda k: (k, 0)),
            pl.BlockSpec((ROWS_DEV // NB, NB), whole),
            pl.BlockSpec((1, SK), whole),
        ],
        out_specs=[pl.BlockSpec((UNITS, TALL, NB), lambda k: (0, 0, 0))] * 2,
        scratch_shapes=[
            V((SK, depth), BF16),
            V((SK, NB), jnp.int32),
            V((SK, N), F32),
            V((N, N + NRHS), F32),
            V((2, 8, NB, NB), F32),
        ],
        compiler_params=pltpu.CompilerParams(vmem_limit_bytes=32 * MIB),
        name="terms",
    )(*map(in_hbm, (matrix, targets, sign_bits.reshape(ROWS_DEV // NB, NB), picked_rows)))


def other_core(v):
    return lax.ppermute(v, "grp", [(i, i ^ 1) for i in range(8)])


def device(g, y, z):
    return g * 32 + y * 8 + z


def over_near(v):
    groups = [
        [device(2 * x + c, y, 2 * far + near) for x in range(4) for y in range(4) for near in range(2)]
        for c in range(2)
        for far in range(4)
    ]
    return lax.all_to_all(v, ("grp", "row"), 0, 0, axis_index_groups=groups, tiled=True)


def over_far(v):
    groups = [[8 * y + 2 * far + near for far in range(4)] for y in range(4) for near in range(2)]
    return lax.all_to_all(v, "row", 0, 0, axis_index_groups=groups, tiled=True)


def summed(keep, send):
    v = (keep + other_core(send)).reshape(32, 4, TALL, NB)
    v = jnp.sum(over_near(v), axis=0)
    v = jnp.sum(over_far(jnp.broadcast_to(v, (4, 4, TALL, NB))), axis=0)
    v = over_near(jnp.broadcast_to(v, (32, 4, TALL, NB)))
    return v.reshape(UNITS, TALL, NB)


def gram_body(in_ref, out_ref, s_ref):
    def take(r, _):
        for c in range(4):
            s_ref[pl.ds(pl.multiple_of(r * 16, 16), 16), c * NB : (c + 1) * NB] = in_ref[pl.ds(r * 4 + c, 1), :16, :][0]
        out_ref[pl.ds(pl.multiple_of(len(LOWER) * NB + r * 32, 32), 32), :] = in_ref[pl.ds(r * 4, 4), 16:, :].reshape(32, NB)
        return 0

    lax.fori_loop(0, 32, take, 0)
    hi, lo = split(s_ref[...])
    hit, lot = hi.T, lo.T
    for i in range(4):
        rows, wide = slice(i * NB, (i + 1) * NB), (i + 1) * NB
        g = dot(hit[rows], hi[:, :wide]) + (dot(hit[rows], lo[:, :wide]) + dot(lot[rows], hi[:, :wide]))
        for j in range(i + 1):
            b = LOWER.index((i, j))
            out_ref[b * NB : (b + 1) * NB, :] = g[:, j * NB : (j + 1) * NB]


def gram(v):
    return pl.pallas_call(
        gram_body,
        out_shape=shape((len(LOWER) + 8) * NB, NB),
        in_specs=[pl.BlockSpec(memory_space=V)],
        out_specs=pl.BlockSpec(memory_space=V),
        scratch_shapes=[V((SK // 2, N), F32)],
        compiler_params=pltpu.CompilerParams(vmem_limit_bytes=16 * MIB),
        name="gram",
    )(v)


def rows_of(v, k):
    return jnp.broadcast_to(v[k : k + 1, :], (8, v.shape[1]))


def lanes_of(v, j):
    return jnp.broadcast_to(v[:, j : j + 1], (8, NB))


def factor_block(d_ref, b_ref, u_ref, w_ref):
    lane = lax.broadcasted_iota(jnp.int32, (8, NB), 1)
    sub = lax.broadcasted_iota(jnp.int32, (8, NB), 0)

    def packed(vs):
        v = vs[0]
        for m in range(1, 8):
            v = jnp.where(sub == m, vs[m], v)
        return v

    for p in range(NB // 8):
        q = 8 * p
        cols = [lanes_of(d_ref[q : q + 8, :], q + m) for m in range(8)]
        s = {(k, m): rows_of(cols[m], k) for m in range(8) for k in range(m, 8)}
        l, r = {}, {}
        for m in range(8):
            r[m] = lax.rsqrt(s[m, m])
            for k in range(m + 1, 8):
                l[k, m] = s[k, m] * r[m]
            for k in range(m + 1, 8):
                for j in range(m + 1, k + 1):
                    s[k, j] = s[k, j] - l[k, m] * l[j, m]

        def forward(vs):
            out = []
            for m in range(8):
                v = vs[m]
                for k in range(m):
                    v = v - l[m, k] * out[k]
                out.append(v * r[m])
            return out

        t, tb = d_ref[q : q + 8, :], b_ref[q : q + 8, :]
        u = forward([rows_of(t, m) for m in range(8)])
        w = forward([rows_of(tb, m) for m in range(8)])
        u_ref[q : q + 8, :] = jnp.where(lane >= q + sub, packed(u), 0.0)
        w_ref[q : q + 8, :] = packed(w)
        for i in range(p + 1, NB // 8):
            o = 8 * i
            v, y = d_ref[o : o + 8, :], b_ref[o : o + 8, :]
            c = forward([lanes_of(v, q + m) for m in range(8)])
            for m in range(8):
                v = v - c[m] * u[m]
                y = y - c[m] * w[m]
            d_ref[o : o + 8, :] = v
            b_ref[o : o + 8, :] = y


def finish_body(
    gram_scale, grad_scale, own_ref, got_ref, a_hbm, t_hbm, l_ref, x_ref, r_hbm,
    a_ref, b_ref, d_ref, db_ref, w_ref, u_ref, lt_ref, li_ref, m_ref, mat_ref, t_ref, r_ref, sems,
):
    fetch = [pltpu.make_async_copy(a_hbm, mat_ref, sems.at[0]), pltpu.make_async_copy(t_hbm, t_ref, sems.at[1])]
    for copy in fetch:
        copy.start()
    zeros = jnp.zeros((NB, NB), F32)
    for b, (i, j) in enumerate(LOWER):
        rows = slice(b * NB, (b + 1) * NB)
        g = (own_ref[rows, :] + got_ref[rows, :]) * gram_scale
        a_ref[i * NB : (i + 1) * NB, j * NB : (j + 1) * NB] = g
        if i != j:
            a_ref[j * NB : (j + 1) * NB, i * NB : (i + 1) * NB] = g.T
    lt_ref[...] = jnp.zeros_like(lt_ref)
    li_ref[...] = jnp.zeros_like(li_ref)
    b_ref[...] = jnp.zeros_like(b_ref)
    row = lax.broadcasted_iota(jnp.int32, (NB, NB), 0)
    eye = (row == lax.broadcasted_iota(jnp.int32, (NB, NB), 1)).astype(F32)

    def block(step, _):
        here = pl.ds(pl.multiple_of(step * NB, NB), NB)
        d_ref[...] = a_ref[here, here]
        db_ref[...] = eye
        factor_block(d_ref, db_ref, u_ref, w_ref)
        lt_ref[here, here] = u_ref[...]
        li_ref[here, here] = w_ref[...]
        for j in range(N // NB):

            @pl.when(step == j)
            def _(j=j):
                o, e = j * NB, (j + 1) * NB
                w = w_ref[...]
                if j:
                    li_ref[o:e, 0:o] = dot_hi(w, b_ref[o:e, 0:o])
                if e < N:
                    u = dot_hi(w, a_ref[o:e, e:])
                    lt_ref[o:e, e:] = u
                    ut = u.T
                    a_ref[e:, e:] = a_ref[e:, e:] - dot_hi(ut, u)
                    b_ref[e:, 0:e] = b_ref[e:, 0:e] - dot_hi(ut, li_ref[o:e, 0:e])

        return 0

    lax.fori_loop(0, N // NB, block, 0)
    l_ref[...] = lt_ref[...].T

    base = len(LOWER) * NB

    def moment(b):
        at = pl.ds(base + (b % 8) * NB, NB)
        mine = own_ref[at, :]
        other = got_ref[at, :]
        return jnp.where(core() == b // 8, mine, other) * grad_scale

    first = jnp.concatenate([moment(i) for i in range(4)], axis=0)
    for b, (i, j) in enumerate(LOWER):
        g = moment(b + 4)
        m_ref[i * NB : (i + 1) * NB, j * NB : (j + 1) * NB] = g
        if i != j:
            m_ref[j * NB : (j + 1) * NB, i * NB : (i + 1) * NB] = g.T

    def times(parts, v):
        hi, lo = split(v)
        both = jnp.concatenate([hi, lo], axis=1)
        ahead, behind = dot(parts[0], both), dot(parts[1], both)
        return ahead[:, :NRHS] + ((ahead[:, NRHS:] + behind[:, :NRHS]) + behind[:, NRHS:])

    inverse, turned, moments = split(li_ref[...]), split(li_ref[...].T), split(m_ref[...])
    x = times(turned, times(inverse, first))
    for _ in range(ITERS - 1):
        x = x + times(turned, times(inverse, first - times(moments, x)))
    x_ref[...] = x
    for copy in fetch:
        copy.wait()
    xs = jnp.concatenate(split(x), axis=1)
    puts = []
    deep = ROWS_DEV // 4
    for c in range(4):
        rows = slice(c * deep, (c + 1) * deep)
        hi, lo = split(mat_ref[rows, :])
        ahead, behind = dot(hi, xs), dot(lo, xs)
        r_ref[rows, :] = t_ref[rows, :] - (ahead[:, :NRHS] + ((ahead[:, NRHS:] + behind[:, :NRHS]) + behind[:, NRHS:]))
        puts.append(pltpu.make_async_copy(r_ref.at[rows, :], r_hbm.at[rows, :], sems.at[2 + c]))
        puts[-1].start()
    for copy in puts:
        copy.wait()


def finished(own, got, matrix, targets, gram_scale, grad_scale):
    def body(*refs):
        finish_body(gram_scale, grad_scale, *refs)

    vmem, hbm = pl.BlockSpec(memory_space=V), pl.BlockSpec(memory_space=pl.ANY)
    return pl.pallas_call(
        body,
        out_shape=[shape(N, N), shape(N, NRHS), shape(ROWS_DEV, NRHS)],
        in_specs=[vmem, vmem, hbm, hbm],
        out_specs=[vmem, vmem, hbm],
        scratch_shapes=[V((N, N), F32)] * 2
        + [V((NB, NB), F32)] * 4
        + [V((N, N), F32)] * 3
        + [V((ROWS_DEV, N), F32)]
        + [V((ROWS_DEV, NRHS), F32)] * 2
        + [pltpu.SemaphoreType.DMA((6,))],
        compiler_params=pltpu.CompilerParams(vmem_limit_bytes=40 * MIB),
        name="finish",
    )(own, got, matrix, targets)


def on_device(matrix, targets, sign_bits, picked_rows):
    total_rows = matrix.shape[0] * lax.axis_size("grp") * lax.axis_size("row")
    keep, send = terms(matrix, targets, sign_bits, picked_rows)
    own = gram(summed(keep, send))
    return tuple(finished(own, other_core(own), matrix, targets, N / (SK * total_rows), N / total_rows))


def solution(mesh):
    rows = P(("grp", "row"), None)
    return jax.shard_map(
        on_device,
        mesh=mesh,
        in_specs=(rows, rows, P(("grp", "row")), rows),
        out_specs=(P(), P(), rows),
        check_vma=False,
    )
```

```python
import jax
import jax.numpy as jnp
from jax import lax
from jax.experimental import pallas as pl
from jax.experimental.pallas import tpu as pltpu
from jax.sharding import PartitionSpec as P

N = 512
NRHS = 128
SK = 1024
ROWS_DEV = 2048
ITERS = 2
NB = 128
UNITS = 128
TALL = 24
HI = lax.Precision.HIGHEST
F32 = jnp.float32
BF16 = jnp.bfloat16
V = pltpu.VMEM
NN = (((1,), (0,)), ((), ()))
TN = (((0,), (0,)), ((), ()))
MIB = 1 << 20
LOWER = [(i, j) for i in range(4) for j in range(i + 1)]


def core():
    return lax.rem(lax.axis_index("grp"), 2)


def shape(*dims):
    return jax.ShapeDtypeStruct(dims, F32)


def split(v):
    hi = v.astype(BF16)
    return hi, (v - hi.astype(F32)).astype(BF16)


def dot(a, b, dims=NN):
    return lax.dot_general(a, b, dims, preferred_element_type=F32)


def dot_hi(a, b, dims=NN):
    return lax.dot_general(a, b, dims, precision=HI, preferred_element_type=F32)


def parity(v, bits):
    shift = 8
    while shift:
        if shift < bits:
            v = v ^ (v >> shift)
        shift //= 2
    return v & 1


def terms_body(a_ref, t_ref, sign_ref, pick_ref, keep_ref, send_ref, base_ref, high_ref, acc_ref, nacc_ref, p_ref):
    k = pl.program_id(0)
    depth = a_ref.shape[0]

    @pl.when(k == 0)
    def _():
        lane = lax.broadcasted_iota(jnp.int32, (NB, depth), 1)
        for b in range(SK // NB):
            row = pick_ref[0:1, b * NB : (b + 1) * NB]
            col = jnp.broadcast_to(row, (NB, NB)).T
            both = jnp.concatenate([col] * (depth // NB), axis=1)
            base_ref[b * NB : (b + 1) * NB, :] = (1 - 2 * parity(both & (depth - 1) & lane, 8)).astype(F32).astype(BF16)
            high_ref[b * NB : (b + 1) * NB, :] = col >> 8
        acc_ref[...] = jnp.zeros_like(acc_ref)
        nacc_ref[...] = jnp.zeros_like(nacc_ref)

    flips = jnp.concatenate([sign_ref[pl.ds(2 * k, 1), :], sign_ref[pl.ds(2 * k + 1, 1), :]], axis=1)
    flips = (1 - 2 * flips).astype(F32)
    hi, lo = split(a_ref[...])
    for b in range(SK // NB):
        rows = slice(b * NB, (b + 1) * NB)
        turn = (1 - 2 * parity(high_ref[rows, :] & k, 4)).astype(F32)
        turn = jnp.concatenate([turn] * (depth // NB), axis=1) * flips
        h = base_ref[rows, :] * turn.astype(BF16)
        acc_ref[rows, :] += dot(h, hi) + dot(h, lo)

    thi, tlo = split(t_ref[...])
    his, los = jnp.concatenate([thi, hi], axis=1), jnp.concatenate([tlo, lo], axis=1)
    hit, lot = hi.T, lo.T
    for i in range(4):
        rows, wide = slice(i * NB, (i + 1) * NB), (i + 2) * NB
        nacc_ref[rows, :wide] += dot(hit[rows], his[:, :wide]) + (dot(hit[rows], los[:, :wide]) + dot(lot[rows], his[:, :wide]))

    @pl.when(k == pl.num_programs(0) - 1)
    def _():
        for i in range(4):
            p_ref[0, i] = nacc_ref[i * NB : (i + 1) * NB, :NB]
        for b, (i, j) in enumerate(LOWER):
            p_ref[(b + 4) // 8, (b + 4) % 8] = nacc_ref[i * NB : (i + 1) * NB, (j + 1) * NB : (j + 2) * NB]
        p_ref[1, 6:] = jnp.zeros_like(p_ref[1, 6:])
        for out, half in ((keep_ref, core()), (send_ref, 1 - core())):

            def put(r, _, out=out, half=half):
                rows = acc_ref[pl.ds(pl.multiple_of(half * (SK // 2) + r * 16, 16), 16), :]
                for c in range(4):
                    out[pl.ds(r * 4 + c, 1), :16, :] = rows[:, c * NB : (c + 1) * NB][None]
                block = p_ref[pl.ds(half, 1), pl.ds(r // 4, 1), pl.ds(pl.multiple_of(lax.rem(r, 4) * 32, 32), 32), :]
                out[pl.ds(r * 4, 4), 16:, :] = block.reshape(4, 8, NB)
                return 0

            lax.fori_loop(0, 32, put, 0)


def in_hbm(v):
    return pltpu.with_memory_space_constraint(v, pltpu.HBM)


def terms(matrix, targets, sign_bits, picked_rows):
    depth = 256
    whole = lambda k: (0, 0)
    return pl.pallas_call(
        terms_body,
        out_shape=[shape(UNITS, TALL, NB)] * 2,
        grid=(ROWS_DEV // depth,),
        in_specs=[
            pl.BlockSpec((depth, N), lambda k: (k, 0)),
            pl.BlockSpec((depth, NRHS), lambda k: (k, 0)),
            pl.BlockSpec((ROWS_DEV // NB, NB), whole),
            pl.BlockSpec((1, SK), whole),
        ],
        out_specs=[pl.BlockSpec((UNITS, TALL, NB), lambda k: (0, 0, 0))] * 2,
        scratch_shapes=[
            V((SK, depth), BF16),
            V((SK, NB), jnp.int32),
            V((SK, N), F32),
            V((N, N + NRHS), F32),
            V((2, 8, NB, NB), F32),
        ],
        compiler_params=pltpu.CompilerParams(vmem_limit_bytes=32 * MIB),
        name="terms",
    )(*map(in_hbm, (matrix, targets, sign_bits.reshape(ROWS_DEV // NB, NB), picked_rows)))


def other_core(v):
    return lax.ppermute(v, "grp", [(i, i ^ 1) for i in range(8)])


def device(g, y, z):
    return g * 32 + y * 8 + z


def over_near(v):
    groups = [
        [device(2 * x + c, y, 2 * far + near) for x in range(4) for y in range(4) for near in range(2)]
        for c in range(2)
        for far in range(4)
    ]
    return lax.all_to_all(v, ("grp", "row"), 0, 0, axis_index_groups=groups, tiled=True)


def over_far(v):
    groups = [[8 * y + 2 * far + near for far in range(4)] for y in range(4) for near in range(2)]
    return lax.all_to_all(v, "row", 0, 0, axis_index_groups=groups, tiled=True)


def summed(keep, send):
    v = (keep + other_core(send)).reshape(32, 4, TALL, NB)
    v = jnp.sum(over_near(v), axis=0)
    v = jnp.sum(over_far(jnp.broadcast_to(v, (4, 4, TALL, NB))), axis=0)
    v = over_near(jnp.broadcast_to(v, (32, 4, TALL, NB)))
    return v.reshape(UNITS, TALL, NB)


def gram_body(in_ref, out_ref, s_ref):
    def take(r, _):
        for c in range(4):
            s_ref[pl.ds(pl.multiple_of(r * 16, 16), 16), c * NB : (c + 1) * NB] = in_ref[pl.ds(r * 4 + c, 1), :16, :][0]
        out_ref[pl.ds(pl.multiple_of(len(LOWER) * NB + r * 32, 32), 32), :] = in_ref[pl.ds(r * 4, 4), 16:, :].reshape(32, NB)
        return 0

    lax.fori_loop(0, 32, take, 0)
    hi, lo = split(s_ref[...])
    hit, lot = hi.T, lo.T
    for i in range(4):
        rows, wide = slice(i * NB, (i + 1) * NB), (i + 1) * NB
        g = dot(hit[rows], hi[:, :wide]) + (dot(hit[rows], lo[:, :wide]) + dot(lot[rows], hi[:, :wide]))
        for j in range(i + 1):
            b = LOWER.index((i, j))
            out_ref[b * NB : (b + 1) * NB, :] = g[:, j * NB : (j + 1) * NB]


def gram(v):
    return pl.pallas_call(
        gram_body,
        out_shape=shape((len(LOWER) + 8) * NB, NB),
        in_specs=[pl.BlockSpec(memory_space=V)],
        out_specs=pl.BlockSpec(memory_space=V),
        scratch_shapes=[V((SK // 2, N), F32)],
        compiler_params=pltpu.CompilerParams(vmem_limit_bytes=16 * MIB),
        name="gram",
    )(v)


def rows_of(v, k):
    return jnp.broadcast_to(v[k : k + 1, :], (8, v.shape[1]))


def lanes_of(v, j):
    return jnp.broadcast_to(v[:, j : j + 1], (8, NB))


def tree(vs):
    while len(vs) > 1:
        vs = [vs[i] + vs[i + 1] for i in range(0, len(vs) - 1, 2)] + ([vs[-1]] if len(vs) % 2 else [])
    return vs[0]


def factor_block(block, u_ref, w_ref):
    lane = lax.broadcasted_iota(jnp.int32, (8, NB), 1)
    sub = lax.broadcasted_iota(jnp.int32, (8, NB), 0)

    def packed(vs):
        v = vs[0]
        for m in range(1, 8):
            v = jnp.where(sub == m, vs[m], v)
        return v

    tiles = list(block)
    last = NB // 8 - 1
    cols = [lanes_of(tiles[0], m) for m in range(8)]
    for p in range(last + 1):
        q = 8 * p
        t = tiles[p]
        s = {(k, m): rows_of(cols[m], k) for m in range(8) for k in range(m, 8)}
        inside = (lane >= q) & (lane < q + 8)
        own = jnp.where(inside, jnp.where(lane == q + sub, 1.0, 0.0), t)
        own = [rows_of(own, m) for m in range(8)]
        close = [i for i in (p + 1, p + 2) if i <= last]
        near = {i: [lanes_of(tiles[i], q + m) for m in range(8)] for i in close}
        ahead = [lanes_of(tiles[p + 1], q + 8 + m) for m in range(8)] if close else None
        l, r, u = {}, {}, []
        c = {i: [] for i in close}
        for m in range(8):
            r[m] = lax.rsqrt(s[m, m])
            for k in range(m + 1, 8):
                l[k, m] = s[k, m] * r[m]
            for k in range(m + 1, 8):
                for j in range(m + 1, k + 1):
                    s[k, j] = s[k, j] - l[k, m] * l[j, m]
            for i in close:
                c[i].append(near[i][m] * r[m])
                for k in range(m + 1, 8):
                    near[i][k] = near[i][k] - l[k, m] * c[i][m]
            if close:
                ahead = [ahead[n] - c[p + 1][m] * rows_of(c[p + 1][m], n) for n in range(8)]
            u.append(own[m] * r[m])
            for k in range(m + 1, 8):
                own[k] = own[k] - l[k, m] * u[m]
        for i in close:
            cleared = jnp.where(inside, 0.0, tiles[i])
            tiles[i] = cleared - tree([c[i][m] * u[m] for m in range(8)])
        cols = ahead
        flat = packed(u)
        w_ref[q : q + 8, :] = jnp.where(lane < q + 8, flat, 0.0)
        diag = jnp.where(lane >= q + 8, flat, 0.0)
        for m in range(8):
            diag = jnp.where((lane == q + m) & (sub == m), r[m] * s[m, m], diag)
            for k in range(m + 1, 8):
                diag = jnp.where((lane == q + k) & (sub == m), l[k, m], diag)
        u_ref[q : q + 8, :] = diag
        if p + 3 <= last:
            z = [None] * 8
            for m in range(7, -1, -1):
                v = u[m]
                for k in range(m + 1, 8):
                    v = v - l[k, m] * z[k]
                z[m] = v * r[m]
            for i in range(p + 3, last + 1):
                v = tiles[i]
                cleared = jnp.where(inside, 0.0, v)
                tiles[i] = cleared - tree([lanes_of(v, q + m) * z[m] for m in range(8)])


def finish_body(
    gram_scale, grad_scale, own_ref, got_ref, mat_ref, t_ref, l_ref, x_ref, r_hbm,
    a_ref, b_ref, lt_ref, li_ref, m_ref, r_ref, sems,
):
    for b, (i, j) in enumerate(LOWER):
        rows = slice(b * NB, (b + 1) * NB)
        g = (own_ref[rows, :] + got_ref[rows, :]) * gram_scale
        a_ref[j * NB : (j + 1) * NB, i * NB : (i + 1) * NB] = g.T if i != j else g
    for i, j in LOWER:
        if i != j:
            zeros = jnp.zeros((NB, NB), F32)
            lt_ref[i * NB : (i + 1) * NB, j * NB : (j + 1) * NB] = zeros
            li_ref[j * NB : (j + 1) * NB, i * NB : (i + 1) * NB] = zeros
    for j in range(N // NB):
        o, e, f = j * NB, (j + 1) * NB, (j + 2) * NB
        tiles = [a_ref[o + 8 * i : o + 8 * i + 8, o:e] for i in range(NB // 8)]
        factor_block(tiles, lt_ref.at[o:e, o:e], li_ref.at[o:e, o:e])
        w = li_ref[o:e, o:e]
        if e < N:
            u = dot_hi(w, a_ref[o:e, e:f])
            ut = u.T
            lt_ref[o:e, e:f] = u
            a_ref[e:f, e:f] = a_ref[e:f, e:f] - dot_hi(ut, u)
        if j:
            li_ref[o:e, 0:o] = dot_hi(w, b_ref[o:e, 0:o])
        if f < N:
            rest = dot_hi(w, a_ref[o:e, f:])
            lt_ref[o:e, f:] = rest
            a_ref[e:f, f:] = a_ref[e:f, f:] - dot_hi(ut, rest)
            for g in range(f, N, NB):
                h = g + NB
                a_ref[g:h, g:] = a_ref[g:h, g:] - dot_hi(lt_ref[o:e, g:h].T, lt_ref[o:e, g:])
        for g in range(e, N, NB):
            h = g + NB
            new = dot_hi(ut if g == e else lt_ref[o:e, g:h].T, li_ref[o:e, 0:e])
            if j:
                b_ref[g:h, 0:o] = b_ref[g:h, 0:o] - new[:, :o]
            b_ref[g:h, o:e] = -new[:, o:]
    l_ref[...] = lt_ref[...].T

    base = len(LOWER) * NB

    def moment(b):
        at = pl.ds(base + (b % 8) * NB, NB)
        mine = own_ref[at, :]
        other = got_ref[at, :]
        return jnp.where(core() == b // 8, mine, other) * grad_scale

    first = jnp.concatenate([moment(i) for i in range(4)], axis=0)
    for b, (i, j) in enumerate(LOWER):
        g = moment(b + 4)
        m_ref[i * NB : (i + 1) * NB, j * NB : (j + 1) * NB] = g
        if i != j:
            m_ref[j * NB : (j + 1) * NB, i * NB : (i + 1) * NB] = g.T

    def times(parts, v):
        hi, lo = split(v)
        both = jnp.concatenate([hi, lo], axis=1)
        ahead, behind = dot(parts[0], both), dot(parts[1], both)
        return ahead[:, :NRHS] + ((ahead[:, NRHS:] + behind[:, :NRHS]) + behind[:, NRHS:])

    inverse, turned, moments = split(li_ref[...]), split(li_ref[...].T), split(m_ref[...])
    x = times(turned, times(inverse, first))
    for _ in range(ITERS - 1):
        x = x + times(turned, times(inverse, first - times(moments, x)))
    x_ref[...] = x
    xs = jnp.concatenate(split(x), axis=1)
    puts = []
    deep = ROWS_DEV // 4
    for c in range(4):
        rows = slice(c * deep, (c + 1) * deep)
        hi, lo = split(mat_ref[rows, :])
        ahead, behind = dot(hi, xs), dot(lo, xs)
        r_ref[rows, :] = t_ref[rows, :] - (ahead[:, :NRHS] + ((ahead[:, NRHS:] + behind[:, :NRHS]) + behind[:, NRHS:]))
        puts.append(pltpu.make_async_copy(r_ref.at[rows, :], r_hbm.at[rows, :], sems.at[c]))
        puts[-1].start()
    for copy in puts:
        copy.wait()


def finished(own, got, matrix, targets, gram_scale, grad_scale):
    def body(*refs):
        finish_body(gram_scale, grad_scale, *refs)

    vmem, hbm = pl.BlockSpec(memory_space=V), pl.BlockSpec(memory_space=pl.ANY)
    return pl.pallas_call(
        body,
        out_shape=[shape(N, N), shape(N, NRHS), shape(ROWS_DEV, NRHS)],
        in_specs=[vmem] * 4,
        out_specs=[vmem, vmem, hbm],
        scratch_shapes=[V((N, N), F32)] * 5 + [V((ROWS_DEV, NRHS), F32), pltpu.SemaphoreType.DMA((4,))],
        compiler_params=pltpu.CompilerParams(vmem_limit_bytes=32 * MIB),
        name="finish",
    )(own, got, matrix, targets)


def on_device(matrix, targets, sign_bits, picked_rows):
    total_rows = matrix.shape[0] * lax.axis_size("grp") * lax.axis_size("row")
    keep, send = terms(matrix, targets, sign_bits, picked_rows)
    own = gram(summed(keep, send))
    return tuple(finished(own, other_core(own), matrix, targets, N / (SK * total_rows), N / total_rows))


def solution(mesh):
    rows = P(("grp", "row"), None)
    return jax.shard_map(
        on_device,
        mesh=mesh,
        in_specs=(rows, rows, P(("grp", "row")), rows),
        out_specs=(P(), P(), rows),
        check_vma=False,
    )
```

```python
import jax
import jax.numpy as jnp
from jax import lax
from jax.experimental import pallas as pl
from jax.experimental.pallas import tpu as pltpu
from jax.sharding import PartitionSpec as P

N = 512
NRHS = 128
SK = 1024
ROWS_DEV = 2048
ITERS = 2
NB = 128
UNITS = 128
TALL = 24
HI = lax.Precision.HIGHEST
F32 = jnp.float32
BF16 = jnp.bfloat16
V = pltpu.VMEM
NN = (((1,), (0,)), ((), ()))
TN = (((0,), (0,)), ((), ()))
MIB = 1 << 20
LOWER = [(i, j) for i in range(4) for j in range(i + 1)]


def core():
    return lax.rem(lax.axis_index("grp"), 2)


def shape(*dims):
    return jax.ShapeDtypeStruct(dims, F32)


def split(v):
    hi = v.astype(BF16)
    return hi, (v - hi.astype(F32)).astype(BF16)


def dot(a, b, dims=NN):
    return lax.dot_general(a, b, dims, preferred_element_type=F32)


def dot_hi(a, b, dims=NN):
    return lax.dot_general(a, b, dims, precision=HI, preferred_element_type=F32)


def parity(v, bits):
    shift = 8
    while shift:
        if shift < bits:
            v = v ^ (v >> shift)
        shift //= 2
    return v & 1


def terms_body(a_ref, t_ref, sign_ref, pick_ref, keep_ref, send_ref, base_ref, high_ref, h_ref, acc_ref, nacc_ref, p_ref):
    k = pl.program_id(0)
    depth = a_ref.shape[0]

    @pl.when(k == 0)
    def _():
        lane = lax.broadcasted_iota(jnp.int32, (NB, depth), 1)
        for b in range(SK // NB):
            row = pick_ref[0:1, b * NB : (b + 1) * NB]
            col = jnp.broadcast_to(row, (NB, NB)).T
            both = jnp.concatenate([col] * (depth // NB), axis=1)
            base_ref[b * NB : (b + 1) * NB, :] = (1 - 2 * parity(both & (depth - 1) & lane, 8)).astype(F32).astype(BF16)
            high_ref[b * NB : (b + 1) * NB, :] = col >> 8
        acc_ref[...] = jnp.zeros_like(acc_ref)
        nacc_ref[...] = jnp.zeros_like(nacc_ref)

    flips = jnp.concatenate([sign_ref[pl.ds(2 * k, 1), :], sign_ref[pl.ds(2 * k + 1, 1), :]], axis=1)
    flips = (1 - 2 * flips).astype(F32)
    hi, lo = split(a_ref[...])
    for b in range(SK // NB):
        rows = slice(b * NB, (b + 1) * NB)
        turn = (1 - 2 * parity(high_ref[rows, :] & k, 4)).astype(F32)
        turn = jnp.concatenate([turn] * (depth // NB), axis=1) * flips
        h_ref[rows, :] = base_ref[rows, :] * turn.astype(BF16)
    h = jnp.concatenate([h_ref[...]] * 2, axis=1)
    both = jnp.concatenate([hi, lo], axis=0)
    for c in (0, N // 2):
        acc_ref[:, c : c + N // 2] += dot(h, both[:, c : c + N // 2])

    thi, tlo = split(t_ref[...])
    his, los = jnp.concatenate([thi, hi], axis=1), jnp.concatenate([tlo, lo], axis=1)
    right = jnp.concatenate([his, los, his], axis=0)
    hit, lot = hi.T, lo.T
    left = jnp.concatenate([hit, hit, lot], axis=1)
    for top, c, e in ((0, 0, 2 * NB), (NB, 2 * NB, 4 * NB), (3 * NB, 4 * NB, 5 * NB)):
        nacc_ref[top:, c:e] += dot(left[top:], right[:, c:e])

    @pl.when(k == pl.num_programs(0) - 1)
    def _():
        for i in range(4):
            p_ref[0, i] = nacc_ref[i * NB : (i + 1) * NB, :NB]
        for b, (i, j) in enumerate(LOWER):
            p_ref[(b + 4) // 8, (b + 4) % 8] = nacc_ref[i * NB : (i + 1) * NB, (j + 1) * NB : (j + 2) * NB]
        p_ref[1, 6:] = jnp.zeros_like(p_ref[1, 6:])
        for out, half in ((keep_ref, core()), (send_ref, 1 - core())):

            def put(r, _, out=out, half=half):
                rows = acc_ref[pl.ds(pl.multiple_of(half * (SK // 2) + r * 16, 16), 16), :]
                for c in range(4):
                    out[pl.ds(r * 4 + c, 1), :16, :] = rows[:, c * NB : (c + 1) * NB][None]
                block = p_ref[pl.ds(half, 1), pl.ds(r // 4, 1), pl.ds(pl.multiple_of(lax.rem(r, 4) * 32, 32), 32), :]
                out[pl.ds(r * 4, 4), 16:, :] = block.reshape(4, 8, NB)
                return 0

            lax.fori_loop(0, 32, put, 0)


def in_hbm(v):
    return pltpu.with_memory_space_constraint(v, pltpu.HBM)


def terms(matrix, targets, sign_bits, picked_rows):
    depth = 256
    whole = lambda k: (0, 0)
    return pl.pallas_call(
        terms_body,
        out_shape=[shape(UNITS, TALL, NB)] * 2,
        grid=(ROWS_DEV // depth,),
        in_specs=[
            pl.BlockSpec((depth, N), lambda k: (k, 0)),
            pl.BlockSpec((depth, NRHS), lambda k: (k, 0)),
            pl.BlockSpec((ROWS_DEV // NB, NB), whole),
            pl.BlockSpec((1, SK), whole),
        ],
        out_specs=[pl.BlockSpec((UNITS, TALL, NB), lambda k: (0, 0, 0))] * 2,
        scratch_shapes=[
            V((SK, depth), BF16),
            V((SK, NB), jnp.int32),
            V((SK, depth), BF16),
            V((SK, N), F32),
            V((N, N + NRHS), F32),
            V((2, 8, NB, NB), F32),
        ],
        compiler_params=pltpu.CompilerParams(vmem_limit_bytes=32 * MIB),
        name="terms",
    )(*map(in_hbm, (matrix, targets, sign_bits.reshape(ROWS_DEV // NB, NB), picked_rows)))


def other_core(v):
    return lax.ppermute(v, "grp", [(i, i ^ 1) for i in range(8)])


def device(g, y, z):
    return g * 32 + y * 8 + z


def over_near(v):
    groups = [
        [device(2 * x + c, y, 2 * far + near) for x in range(4) for y in range(4) for near in range(2)]
        for c in range(2)
        for far in range(4)
    ]
    return lax.all_to_all(v, ("grp", "row"), 0, 0, axis_index_groups=groups, tiled=True)


def over_far(v):
    groups = [[8 * y + 2 * far + near for far in range(4)] for y in range(4) for near in range(2)]
    return lax.all_to_all(v, "row", 0, 0, axis_index_groups=groups, tiled=True)


def summed(keep, send):
    v = (keep + other_core(send)).reshape(32, 4, TALL, NB)
    v = jnp.sum(over_near(v), axis=0)
    v = jnp.sum(over_far(jnp.broadcast_to(v, (4, 4, TALL, NB))), axis=0)
    v = over_near(jnp.broadcast_to(v, (32, 4, TALL, NB)))
    return v.reshape(UNITS, TALL, NB)


def gram_body(in_ref, out_ref, s_ref):
    def take(r, _):
        for c in range(4):
            s_ref[pl.ds(pl.multiple_of(r * 16, 16), 16), c * NB : (c + 1) * NB] = in_ref[pl.ds(r * 4 + c, 1), :16, :][0]
        out_ref[pl.ds(pl.multiple_of(len(LOWER) * NB + r * 32, 32), 32), :] = in_ref[pl.ds(r * 4, 4), 16:, :].reshape(32, NB)
        return 0

    lax.fori_loop(0, 32, take, 0)
    hi, lo = split(s_ref[...])
    hit, lot = hi.T, lo.T
    for i in range(4):
        rows, wide = slice(i * NB, (i + 1) * NB), (i + 1) * NB
        g = dot(hit[rows], hi[:, :wide]) + (dot(hit[rows], lo[:, :wide]) + dot(lot[rows], hi[:, :wide]))
        for j in range(i + 1):
            b = LOWER.index((i, j))
            out_ref[b * NB : (b + 1) * NB, :] = g[:, j * NB : (j + 1) * NB]


def gram(v):
    return pl.pallas_call(
        gram_body,
        out_shape=shape((len(LOWER) + 8) * NB, NB),
        in_specs=[pl.BlockSpec(memory_space=V)],
        out_specs=pl.BlockSpec(memory_space=V),
        scratch_shapes=[V((SK // 2, N), F32)],
        compiler_params=pltpu.CompilerParams(vmem_limit_bytes=16 * MIB),
        name="gram",
    )(v)


def rows_of(v, k):
    return jnp.broadcast_to(v[k : k + 1, :], (8, v.shape[1]))


def lanes_of(v, j):
    return jnp.broadcast_to(v[:, j : j + 1], (8, NB))


def tree(vs):
    while len(vs) > 1:
        vs = [vs[i] + vs[i + 1] for i in range(0, len(vs) - 1, 2)] + ([vs[-1]] if len(vs) % 2 else [])
    return vs[0]


def factor_block(block, u_ref, d_ref, w_ref):
    lane = lax.broadcasted_iota(jnp.int32, (8, NB), 1)
    sub = lax.broadcasted_iota(jnp.int32, (8, NB), 0)

    def packed(vs):
        v = vs[0]
        for m in range(1, 8):
            v = jnp.where(sub == m, vs[m], v)
        return v

    tiles = list(block)
    last = NB // 8 - 1
    cols = [lanes_of(tiles[0], m) for m in range(8)]
    for p in range(last + 1):
        q = 8 * p
        t = tiles[p]
        inside = (lane >= q) & (lane < q + 8)
        own = jnp.where(inside, jnp.where(lane == q + sub, 1.0, 0.0), t)
        own = [rows_of(own, m) for m in range(8)]
        close = [i for i in (p + 1, p + 2) if i <= last]
        near = {i: [lanes_of(tiles[i], q + m) for m in range(8)] for i in close}
        ahead = [lanes_of(tiles[p + 1], q + 8 + m) for m in range(8)] if close else None
        l, r, u = {}, {}, []
        c = {i: [] for i in close}
        diag = jnp.zeros((8, NB), F32)
        for m in range(8):
            pivot = rows_of(cols[m], m)
            r[m] = lax.rsqrt(pivot)
            low = cols[m] * r[m]
            diag = jnp.where(lane == q + m, low, diag)
            for k in range(m + 1, 8):
                l[k, m] = rows_of(low, k)
                cols[k] = cols[k] - low * l[k, m]
            for i in close:
                c[i].append(near[i][m] * r[m])
                for k in range(m + 1, 8):
                    near[i][k] = near[i][k] - l[k, m] * c[i][m]
            if close:
                ahead = [ahead[n] - c[p + 1][m] * rows_of(c[p + 1][m], n) for n in range(8)]
            u.append(own[m] * r[m])
            for k in range(m + 1, 8):
                own[k] = own[k] - l[k, m] * u[m]
        for i in close:
            cleared = jnp.where(inside, 0.0, tiles[i])
            tiles[i] = cleared - tree([c[i][m] * u[m] for m in range(8)])
        cols = ahead
        flat = packed(u)
        w_ref[q : q + 8, :] = jnp.where(lane < q + 8, flat, 0.0)
        u_ref[q : q + 8, :] = jnp.where(lane >= q + 8, flat, 0.0)
        d_ref[q : q + 8, :] = jnp.where(q + sub >= lane, diag, 0.0)
        if p + 3 <= last:
            z = [None] * 8
            for m in range(7, -1, -1):
                v = u[m]
                for k in range(m + 1, 8):
                    v = v - l[k, m] * z[k]
                z[m] = v * r[m]
            for i in range(p + 3, last + 1):
                v = tiles[i]
                cleared = jnp.where(inside, 0.0, v)
                tiles[i] = cleared - tree([lanes_of(v, q + m) * z[m] for m in range(8)])


def finish_body(
    gram_scale, grad_scale, own_ref, got_ref, mat_ref, t_ref, l_ref, x_ref, r_hbm,
    a_ref, b_ref, lt_ref, li_ref, m_ref, d_ref, r_ref, sems,
):
    for b, (i, j) in enumerate(LOWER):
        rows = slice(b * NB, (b + 1) * NB)
        g = (own_ref[rows, :] + got_ref[rows, :]) * gram_scale
        a_ref[j * NB : (j + 1) * NB, i * NB : (i + 1) * NB] = g.T if i != j else g
    for i, j in LOWER:
        if i != j:
            zeros = jnp.zeros((NB, NB), F32)
            lt_ref[i * NB : (i + 1) * NB, j * NB : (j + 1) * NB] = zeros
            li_ref[j * NB : (j + 1) * NB, i * NB : (i + 1) * NB] = zeros
    for j in range(N // NB):
        o, e, f = j * NB, (j + 1) * NB, (j + 2) * NB
        tiles = [a_ref[o + 8 * i : o + 8 * i + 8, o:e] for i in range(NB // 8)]
        factor_block(tiles, lt_ref.at[o:e, o:e], d_ref.at[o:e, :], li_ref.at[o:e, o:e])
        w = li_ref[o:e, o:e]
        if e < N:
            u = dot_hi(w, a_ref[o:e, e:f])
            ut = u.T
            lt_ref[o:e, e:f] = u
            a_ref[e:f, e:f] = a_ref[e:f, e:f] - dot_hi(ut, u)
        if j:
            li_ref[o:e, 0:o] = dot_hi(w, b_ref[o:e, 0:o])
        if f < N:
            rest = dot_hi(w, a_ref[o:e, f:])
            lt_ref[o:e, f:] = rest
            a_ref[e:f, f:] = a_ref[e:f, f:] - dot_hi(ut, rest)
            for g in range(f, N, NB):
                h = g + NB
                a_ref[g:h, g:] = a_ref[g:h, g:] - dot_hi(lt_ref[o:e, g:h].T, lt_ref[o:e, g:])
        for g in range(e, N, NB):
            h = g + NB
            new = dot_hi(ut if g == e else lt_ref[o:e, g:h].T, li_ref[o:e, 0:e])
            if j:
                b_ref[g:h, 0:o] = b_ref[g:h, 0:o] - new[:, :o]
            b_ref[g:h, o:e] = -new[:, o:]
    l_ref[...] = lt_ref[...].T
    for o in range(0, N, NB):
        e = o + NB
        l_ref[o:e, o:e] = lt_ref[o:e, o:e].T + d_ref[o:e, :]

    base = len(LOWER) * NB

    def moment(b):
        at = pl.ds(base + (b % 8) * NB, NB)
        mine = own_ref[at, :]
        other = got_ref[at, :]
        return jnp.where(core() == b // 8, mine, other) * grad_scale

    first = jnp.concatenate([moment(i) for i in range(4)], axis=0)
    for b, (i, j) in enumerate(LOWER):
        g = moment(b + 4)
        m_ref[i * NB : (i + 1) * NB, j * NB : (j + 1) * NB] = g
        if i != j:
            m_ref[j * NB : (j + 1) * NB, i * NB : (i + 1) * NB] = g.T

    def times(parts, v):
        hi, lo = split(v)
        both = jnp.concatenate([hi, lo], axis=1)
        ahead, behind = dot(parts[0], both), dot(parts[1], both)
        return ahead[:, :NRHS] + ((ahead[:, NRHS:] + behind[:, :NRHS]) + behind[:, NRHS:])

    inverse, turned, moments = split(li_ref[...]), split(li_ref[...].T), split(m_ref[...])
    x = times(turned, times(inverse, first))
    for _ in range(ITERS - 1):
        x = x + times(turned, times(inverse, first - times(moments, x)))
    x_ref[...] = x
    xs = jnp.concatenate(split(x), axis=1)
    puts = []
    deep = ROWS_DEV // 4
    for c in range(4):
        rows = slice(c * deep, (c + 1) * deep)
        hi, lo = split(mat_ref[rows, :])
        ahead, behind = dot(hi, xs), dot(lo, xs)
        r_ref[rows, :] = t_ref[rows, :] - (ahead[:, :NRHS] + ((ahead[:, NRHS:] + behind[:, :NRHS]) + behind[:, NRHS:]))
        puts.append(pltpu.make_async_copy(r_ref.at[rows, :], r_hbm.at[rows, :], sems.at[c]))
        puts[-1].start()
    for copy in puts:
        copy.wait()


def finished(own, got, matrix, targets, gram_scale, grad_scale):
    def body(*refs):
        finish_body(gram_scale, grad_scale, *refs)

    vmem, hbm = pl.BlockSpec(memory_space=V), pl.BlockSpec(memory_space=pl.ANY)
    return pl.pallas_call(
        body,
        out_shape=[shape(N, N), shape(N, NRHS), shape(ROWS_DEV, NRHS)],
        in_specs=[vmem] * 4,
        out_specs=[vmem, vmem, hbm],
        scratch_shapes=[V((N, N), F32)] * 5 + [V((N, NB), F32), V((ROWS_DEV, NRHS), F32), pltpu.SemaphoreType.DMA((4,))],
        compiler_params=pltpu.CompilerParams(vmem_limit_bytes=32 * MIB),
        name="finish",
    )(own, got, matrix, targets)


def on_device(matrix, targets, sign_bits, picked_rows):
    total_rows = matrix.shape[0] * lax.axis_size("grp") * lax.axis_size("row")
    keep, send = terms(matrix, targets, sign_bits, picked_rows)
    own = gram(summed(keep, send))
    return tuple(finished(own, other_core(own), matrix, targets, N / (SK * total_rows), N / total_rows))


def solution(mesh):
    rows = P(("grp", "row"), None)
    return jax.shard_map(
        on_device,
        mesh=mesh,
        in_specs=(rows, rows, P(("grp", "row")), rows),
        out_specs=(P(), P(), rows),
        check_vma=False,
    )
```

```python
import jax
import jax.numpy as jnp
from jax import lax
from jax.experimental import pallas as pl
from jax.experimental.pallas import tpu as pltpu
from jax.sharding import PartitionSpec as P

N = 512
NRHS = 128
SK = 1024
ROWS_DEV = 2048
ITERS = 2
NB = 128
UNITS = 128
TALL = 24
HI = lax.Precision.HIGHEST
F32 = jnp.float32
BF16 = jnp.bfloat16
V = pltpu.VMEM
NN = (((1,), (0,)), ((), ()))
TN = (((0,), (0,)), ((), ()))
MIB = 1 << 20
LOWER = [(i, j) for i in range(4) for j in range(i + 1)]


def core():
    return lax.rem(lax.axis_index("grp"), 2)


def shape(*dims):
    return jax.ShapeDtypeStruct(dims, F32)


def split(v):
    hi = v.astype(BF16)
    return hi, (v - hi.astype(F32)).astype(BF16)


def dot(a, b, dims=NN):
    return lax.dot_general(a, b, dims, preferred_element_type=F32)


def dot_hi(a, b, dims=NN):
    return lax.dot_general(a, b, dims, precision=HI, preferred_element_type=F32)


def dot_parts(a, b):
    (ah, al), (bh, bl) = split(a), split(b)
    return dot(jnp.concatenate([ah, ah, al], axis=1), jnp.concatenate([bh, bl, bh], axis=0))


def parity(v, bits):
    shift = 8
    while shift:
        if shift < bits:
            v = v ^ (v >> shift)
        shift //= 2
    return v & 1


def terms_body(a_ref, t_ref, sign_ref, pick_ref, keep_ref, send_ref, base_ref, high_ref, h_ref, acc_ref, nacc_ref, p_ref):
    k = pl.program_id(0)
    depth = a_ref.shape[0]

    @pl.when(k == 0)
    def _():
        lane = lax.broadcasted_iota(jnp.int32, (NB, depth), 1)
        for b in range(SK // NB):
            row = pick_ref[0:1, b * NB : (b + 1) * NB]
            col = jnp.broadcast_to(row, (NB, NB)).T
            both = jnp.concatenate([col] * (depth // NB), axis=1)
            base_ref[b * NB : (b + 1) * NB, :] = (1 - 2 * parity(both & (depth - 1) & lane, 8)).astype(F32).astype(BF16)
            high_ref[b * NB : (b + 1) * NB, :] = col >> 8
        acc_ref[...] = jnp.zeros_like(acc_ref)
        nacc_ref[...] = jnp.zeros_like(nacc_ref)

    flips = jnp.concatenate([sign_ref[pl.ds(2 * k, 1), :], sign_ref[pl.ds(2 * k + 1, 1), :]], axis=1)
    flips = (1 - 2 * flips).astype(F32)
    hi, lo = split(a_ref[...])
    for b in range(SK // NB):
        rows = slice(b * NB, (b + 1) * NB)
        turn = (1 - 2 * parity(high_ref[rows, :] & k, 4)).astype(F32)
        turn = jnp.concatenate([turn] * (depth // NB), axis=1) * flips
        h_ref[rows, :] = base_ref[rows, :] * turn.astype(BF16)
    h = jnp.concatenate([h_ref[...]] * 2, axis=1)
    both = jnp.concatenate([hi, lo], axis=0)
    for c in (0, N // 2):
        acc_ref[:, c : c + N // 2] += dot(h, both[:, c : c + N // 2])

    thi, tlo = split(t_ref[...])
    his, los = jnp.concatenate([thi, hi], axis=1), jnp.concatenate([tlo, lo], axis=1)
    right = jnp.concatenate([his, los, his], axis=0)
    hit, lot = hi.T, lo.T
    left = jnp.concatenate([hit, hit, lot], axis=1)
    for top, c, e in ((0, 0, 2 * NB), (NB, 2 * NB, 4 * NB), (3 * NB, 4 * NB, 5 * NB)):
        nacc_ref[top:, c:e] += dot(left[top:], right[:, c:e])

    @pl.when(k == pl.num_programs(0) - 1)
    def _():
        for i in range(4):
            p_ref[0, i] = nacc_ref[i * NB : (i + 1) * NB, :NB]
        for b, (i, j) in enumerate(LOWER):
            p_ref[(b + 4) // 8, (b + 4) % 8] = nacc_ref[i * NB : (i + 1) * NB, (j + 1) * NB : (j + 2) * NB]
        p_ref[1, 6:] = jnp.zeros_like(p_ref[1, 6:])
        for out, half in ((keep_ref, core()), (send_ref, 1 - core())):

            def put(r, _, out=out, half=half):
                rows = acc_ref[pl.ds(pl.multiple_of(half * (SK // 2) + r * 16, 16), 16), :]
                for c in range(4):
                    out[pl.ds(r * 4 + c, 1), :16, :] = rows[:, c * NB : (c + 1) * NB][None]
                block = p_ref[pl.ds(half, 1), pl.ds(r // 4, 1), pl.ds(pl.multiple_of(lax.rem(r, 4) * 32, 32), 32), :]
                out[pl.ds(r * 4, 4), 16:, :] = block.reshape(4, 8, NB)
                return 0

            lax.fori_loop(0, 32, put, 0)


def in_hbm(v):
    return pltpu.with_memory_space_constraint(v, pltpu.HBM)


def terms(matrix, targets, sign_bits, picked_rows):
    depth = 256
    whole = lambda k: (0, 0)
    return pl.pallas_call(
        terms_body,
        out_shape=[shape(UNITS, TALL, NB)] * 2,
        grid=(ROWS_DEV // depth,),
        in_specs=[
            pl.BlockSpec((depth, N), lambda k: (k, 0)),
            pl.BlockSpec((depth, NRHS), lambda k: (k, 0)),
            pl.BlockSpec((ROWS_DEV // NB, NB), whole),
            pl.BlockSpec((1, SK), whole),
        ],
        out_specs=[pl.BlockSpec((UNITS, TALL, NB), lambda k: (0, 0, 0))] * 2,
        scratch_shapes=[
            V((SK, depth), BF16),
            V((SK, NB), jnp.int32),
            V((SK, depth), BF16),
            V((SK, N), F32),
            V((N, N + NRHS), F32),
            V((2, 8, NB, NB), F32),
        ],
        compiler_params=pltpu.CompilerParams(vmem_limit_bytes=32 * MIB),
        name="terms",
    )(*map(in_hbm, (matrix, targets, sign_bits.reshape(ROWS_DEV // NB, NB), picked_rows)))


def other_core(v):
    return lax.ppermute(v, "grp", [(i, i ^ 1) for i in range(8)])


def device(g, y, z):
    return g * 32 + y * 8 + z


def over_near(v):
    groups = [
        [device(2 * x + c, y, 2 * far + near) for x in range(4) for y in range(4) for near in range(2)]
        for c in range(2)
        for far in range(4)
    ]
    return lax.all_to_all(v, ("grp", "row"), 0, 0, axis_index_groups=groups, tiled=True)


def over_far(v):
    groups = [[8 * y + 2 * far + near for far in range(4)] for y in range(4) for near in range(2)]
    return lax.all_to_all(v, "row", 0, 0, axis_index_groups=groups, tiled=True)


def summed(keep, send):
    v = (keep + other_core(send)).reshape(32, 4, TALL, NB)
    v = jnp.sum(over_near(v), axis=0)
    v = jnp.sum(over_far(jnp.broadcast_to(v, (4, 4, TALL, NB))), axis=0)
    v = over_near(jnp.broadcast_to(v, (32, 4, TALL, NB)))
    return v.reshape(UNITS, TALL, NB)


def gram_body(in_ref, out_ref, s_ref):
    def take(r, _):
        for c in range(4):
            s_ref[pl.ds(pl.multiple_of(r * 16, 16), 16), c * NB : (c + 1) * NB] = in_ref[pl.ds(r * 4 + c, 1), :16, :][0]
        out_ref[pl.ds(pl.multiple_of(len(LOWER) * NB + r * 32, 32), 32), :] = in_ref[pl.ds(r * 4, 4), 16:, :].reshape(32, NB)
        return 0

    lax.fori_loop(0, 32, take, 0)
    hi, lo = split(s_ref[...])
    hit, lot = hi.T, lo.T
    for i in range(4):
        rows, wide = slice(i * NB, (i + 1) * NB), (i + 1) * NB
        g = dot(hit[rows], hi[:, :wide]) + (dot(hit[rows], lo[:, :wide]) + dot(lot[rows], hi[:, :wide]))
        for j in range(i + 1):
            b = LOWER.index((i, j))
            out_ref[b * NB : (b + 1) * NB, :] = g[:, j * NB : (j + 1) * NB]


def gram(v):
    return pl.pallas_call(
        gram_body,
        out_shape=shape((len(LOWER) + 8) * NB, NB),
        in_specs=[pl.BlockSpec(memory_space=V)],
        out_specs=pl.BlockSpec(memory_space=V),
        scratch_shapes=[V((SK // 2, N), F32)],
        compiler_params=pltpu.CompilerParams(vmem_limit_bytes=16 * MIB),
        name="gram",
    )(v)


def rows_of(v, k):
    return jnp.broadcast_to(v[k : k + 1, :], (8, v.shape[1]))


def lanes_of(v, j):
    return jnp.broadcast_to(v[:, j : j + 1], (8, NB))


def tree(vs):
    while len(vs) > 1:
        vs = [vs[i] + vs[i + 1] for i in range(0, len(vs) - 1, 2)] + ([vs[-1]] if len(vs) % 2 else [])
    return vs[0]


def factor_block(block, u_ref, d_ref, w_ref):
    lane = lax.broadcasted_iota(jnp.int32, (8, NB), 1)
    sub = lax.broadcasted_iota(jnp.int32, (8, NB), 0)

    def packed(vs):
        v = vs[0]
        for m in range(1, 8):
            v = jnp.where(sub == m, vs[m], v)
        return v

    tiles = list(block)
    last = NB // 8 - 1
    cols = [lanes_of(tiles[0], m) for m in range(8)]
    for p in range(last + 1):
        q = 8 * p
        t = tiles[p]
        inside = (lane >= q) & (lane < q + 8)
        own = jnp.where(inside, jnp.where(lane == q + sub, 1.0, 0.0), t)
        own = [rows_of(own, m) for m in range(8)]
        close = [i for i in (p + 1, p + 2) if i <= last]
        near = {i: [lanes_of(tiles[i], q + m) for m in range(8)] for i in close}
        ahead = [lanes_of(tiles[p + 1], q + 8 + m) for m in range(8)] if close else None
        l, r, u = {}, {}, []
        c = {i: [] for i in close}
        diag = jnp.zeros((8, NB), F32)
        for m in range(8):
            pivot = rows_of(cols[m], m)
            r[m] = lax.rsqrt(pivot)
            low = cols[m] * r[m]
            diag = jnp.where(lane == q + m, low, diag)
            for k in range(m + 1, 8):
                l[k, m] = rows_of(low, k)
                cols[k] = cols[k] - low * l[k, m]
            for i in close:
                c[i].append(near[i][m] * r[m])
                for k in range(m + 1, 8):
                    near[i][k] = near[i][k] - l[k, m] * c[i][m]
            if close:
                ahead = [ahead[n] - c[p + 1][m] * rows_of(c[p + 1][m], n) for n in range(8)]
            u.append(own[m] * r[m])
            for k in range(m + 1, 8):
                own[k] = own[k] - l[k, m] * u[m]
        for i in close:
            cleared = jnp.where(inside, 0.0, tiles[i])
            tiles[i] = cleared - tree([c[i][m] * u[m] for m in range(8)])
        cols = ahead
        flat = packed(u)
        w_ref[q : q + 8, :] = jnp.where(lane < q + 8, flat, 0.0)
        u_ref[q : q + 8, :] = jnp.where(lane >= q + 8, flat, 0.0)
        d_ref[q : q + 8, :] = jnp.where(q + sub >= lane, diag, 0.0)
        if p + 3 <= last:
            z = [None] * 8
            for m in range(7, -1, -1):
                v = u[m]
                for k in range(m + 1, 8):
                    v = v - l[k, m] * z[k]
                z[m] = v * r[m]
            for i in range(p + 3, last + 1):
                v = tiles[i]
                cleared = jnp.where(inside, 0.0, v)
                tiles[i] = cleared - tree([lanes_of(v, q + m) * z[m] for m in range(8)])


def finish_body(
    gram_scale, grad_scale, own_ref, got_ref, mat_ref, t_ref, l_ref, x_ref, r_hbm,
    a_ref, b_ref, lt_ref, li_ref, m_ref, d_ref, r_ref, sems,
):
    for b, (i, j) in enumerate(LOWER):
        rows = slice(b * NB, (b + 1) * NB)
        g = (own_ref[rows, :] + got_ref[rows, :]) * gram_scale
        a_ref[j * NB : (j + 1) * NB, i * NB : (i + 1) * NB] = g.T if i != j else g
    for i, j in LOWER:
        if i != j:
            zeros = jnp.zeros((NB, NB), F32)
            lt_ref[i * NB : (i + 1) * NB, j * NB : (j + 1) * NB] = zeros
            li_ref[j * NB : (j + 1) * NB, i * NB : (i + 1) * NB] = zeros
    for j in range(N // NB):
        o, e, f = j * NB, (j + 1) * NB, (j + 2) * NB
        tiles = [a_ref[o + 8 * i : o + 8 * i + 8, o:e] for i in range(NB // 8)]
        factor_block(tiles, lt_ref.at[o:e, o:e], d_ref.at[o:e, :], li_ref.at[o:e, o:e])
        w = li_ref[o:e, o:e]
        if e < N:
            u = dot_hi(w, a_ref[o:e, e:f])
            ut = u.T
            lt_ref[o:e, e:f] = u
            a_ref[e:f, e:f] = a_ref[e:f, e:f] - dot_hi(ut, u)
        if j:
            li_ref[o:e, 0:o] = dot_parts(w, b_ref[o:e, 0:o])
        if f < N:
            rest = dot_hi(w, a_ref[o:e, f:])
            lt_ref[o:e, f:] = rest
            a_ref[e:f, f:] = a_ref[e:f, f:] - dot_hi(ut, rest)
            for g in range(f, N, NB):
                h = g + NB
                a_ref[g:h, g:] = a_ref[g:h, g:] - dot_hi(lt_ref[o:e, g:h].T, lt_ref[o:e, g:])
        for g in range(e, N, NB):
            h = g + NB
            new = dot_parts(ut if g == e else lt_ref[o:e, g:h].T, li_ref[o:e, 0:e])
            if j:
                b_ref[g:h, 0:o] = b_ref[g:h, 0:o] - new[:, :o]
            b_ref[g:h, o:e] = -new[:, o:]
    l_ref[...] = lt_ref[...].T
    for o in range(0, N, NB):
        e = o + NB
        l_ref[o:e, o:e] = lt_ref[o:e, o:e].T + d_ref[o:e, :]

    base = len(LOWER) * NB

    def moment(b):
        at = pl.ds(base + (b % 8) * NB, NB)
        mine = own_ref[at, :]
        other = got_ref[at, :]
        return jnp.where(core() == b // 8, mine, other) * grad_scale

    first = jnp.concatenate([moment(i) for i in range(4)], axis=0)
    for b, (i, j) in enumerate(LOWER):
        g = moment(b + 4)
        m_ref[i * NB : (i + 1) * NB, j * NB : (j + 1) * NB] = g
        if i != j:
            m_ref[j * NB : (j + 1) * NB, i * NB : (i + 1) * NB] = g.T

    def times(parts, v):
        hi, lo = split(v)
        both = jnp.concatenate([hi, lo], axis=1)
        ahead, behind = dot(parts[0], both), dot(parts[1], both)
        return ahead[:, :NRHS] + ((ahead[:, NRHS:] + behind[:, :NRHS]) + behind[:, NRHS:])

    inverse, turned, moments = split(li_ref[...]), split(li_ref[...].T), split(m_ref[...])
    x = times(turned, times(inverse, first))
    for _ in range(ITERS - 1):
        x = x + times(turned, times(inverse, first - times(moments, x)))
    x_ref[...] = x
    xs = jnp.concatenate(split(x), axis=1)
    puts = []
    deep = ROWS_DEV // 4
    for c in range(4):
        rows = slice(c * deep, (c + 1) * deep)
        hi, lo = split(mat_ref[rows, :])
        ahead, behind = dot(hi, xs), dot(lo, xs)
        r_ref[rows, :] = t_ref[rows, :] - (ahead[:, :NRHS] + ((ahead[:, NRHS:] + behind[:, :NRHS]) + behind[:, NRHS:]))
        puts.append(pltpu.make_async_copy(r_ref.at[rows, :], r_hbm.at[rows, :], sems.at[c]))
        puts[-1].start()
    for copy in puts:
        copy.wait()


def finished(own, got, matrix, targets, gram_scale, grad_scale):
    def body(*refs):
        finish_body(gram_scale, grad_scale, *refs)

    vmem, hbm = pl.BlockSpec(memory_space=V), pl.BlockSpec(memory_space=pl.ANY)
    return pl.pallas_call(
        body,
        out_shape=[shape(N, N), shape(N, NRHS), shape(ROWS_DEV, NRHS)],
        in_specs=[vmem] * 4,
        out_specs=[vmem, vmem, hbm],
        scratch_shapes=[V((N, N), F32)] * 5 + [V((N, NB), F32), V((ROWS_DEV, NRHS), F32), pltpu.SemaphoreType.DMA((4,))],
        compiler_params=pltpu.CompilerParams(vmem_limit_bytes=32 * MIB),
        name="finish",
    )(own, got, matrix, targets)


def on_device(matrix, targets, sign_bits, picked_rows):
    total_rows = matrix.shape[0] * lax.axis_size("grp") * lax.axis_size("row")
    keep, send = terms(matrix, targets, sign_bits, picked_rows)
    own = gram(summed(keep, send))
    return tuple(finished(own, other_core(own), matrix, targets, N / (SK * total_rows), N / total_rows))


def solution(mesh):
    rows = P(("grp", "row"), None)
    return jax.shard_map(
        on_device,
        mesh=mesh,
        in_specs=(rows, rows, P(("grp", "row")), rows),
        out_specs=(P(), P(), rows),
        check_vma=False,
    )
```

```python
import jax
import jax.numpy as jnp
from jax import lax
from jax.experimental import pallas as pl
from jax.experimental.pallas import tpu as pltpu
from jax.sharding import PartitionSpec as P

N = 512
NRHS = 128
SK = 1024
ROWS_DEV = 2048
ITERS = 2
NB = 128
UNITS = 128
TALL = 24
HI = lax.Precision.HIGHEST
F32 = jnp.float32
BF16 = jnp.bfloat16
V = pltpu.VMEM
NN = (((1,), (0,)), ((), ()))
TN = (((0,), (0,)), ((), ()))
MIB = 1 << 20
LOWER = [(i, j) for i in range(4) for j in range(i + 1)]


def core():
    return lax.rem(lax.axis_index("grp"), 2)


def shape(*dims):
    return jax.ShapeDtypeStruct(dims, F32)


def split(v):
    hi = v.astype(BF16)
    return hi, (v - hi.astype(F32)).astype(BF16)


def dot(a, b, dims=NN):
    return lax.dot_general(a, b, dims, preferred_element_type=F32)


def dot_hi(a, b, dims=NN):
    return lax.dot_general(a, b, dims, precision=HI, preferred_element_type=F32)


def dot_parts(a, b):
    (ah, al), (bh, bl) = split(a), split(b)
    return dot(jnp.concatenate([ah, ah, al], axis=1), jnp.concatenate([bh, bl, bh], axis=0))


def parity(v, bits):
    shift = 8
    while shift:
        if shift < bits:
            v = v ^ (v >> shift)
        shift //= 2
    return v & 1


def terms_body(a_ref, t_ref, sign_ref, pick_ref, keep_ref, send_ref, base_ref, high_ref, h_ref, acc_ref, nacc_ref, p_ref):
    k = pl.program_id(0)
    depth = a_ref.shape[0]

    @pl.when(k == 0)
    def _():
        lane = lax.broadcasted_iota(jnp.int32, (NB, depth), 1)
        for b in range(SK // NB):
            row = pick_ref[0:1, b * NB : (b + 1) * NB]
            col = jnp.broadcast_to(row, (NB, NB)).T
            both = jnp.concatenate([col] * (depth // NB), axis=1)
            base_ref[b * NB : (b + 1) * NB, :] = (1 - 2 * parity(both & (depth - 1) & lane, 8)).astype(F32).astype(BF16)
            high_ref[b * NB : (b + 1) * NB, :] = col >> 8
        acc_ref[...] = jnp.zeros_like(acc_ref)
        nacc_ref[...] = jnp.zeros_like(nacc_ref)

    flips = jnp.concatenate([sign_ref[pl.ds(2 * k, 1), :], sign_ref[pl.ds(2 * k + 1, 1), :]], axis=1)
    flips = (1 - 2 * flips).astype(F32)
    hi, lo = split(a_ref[...])
    for b in range(SK // NB):
        rows = slice(b * NB, (b + 1) * NB)
        turn = (1 - 2 * parity(high_ref[rows, :] & k, 4)).astype(F32)
        turn = jnp.concatenate([turn] * (depth // NB), axis=1) * flips
        h_ref[rows, :] = base_ref[rows, :] * turn.astype(BF16)
    h = jnp.concatenate([h_ref[...]] * 2, axis=1)
    both = jnp.concatenate([hi, lo], axis=0)
    for c in (0, N // 2):
        acc_ref[:, c : c + N // 2] += dot(h, both[:, c : c + N // 2])

    thi, tlo = split(t_ref[...])
    his, los = jnp.concatenate([thi, hi], axis=1), jnp.concatenate([tlo, lo], axis=1)
    right = jnp.concatenate([his, los, his], axis=0)
    hit, lot = hi.T, lo.T
    left = jnp.concatenate([hit, hit, lot], axis=1)
    for top, c, e in ((0, 0, 2 * NB), (NB, 2 * NB, 4 * NB), (3 * NB, 4 * NB, 5 * NB)):
        nacc_ref[top:, c:e] += dot(left[top:], right[:, c:e])

    @pl.when(k == pl.num_programs(0) - 1)
    def _():
        for i in range(4):
            p_ref[0, i] = nacc_ref[i * NB : (i + 1) * NB, :NB]
        for b, (i, j) in enumerate(LOWER):
            p_ref[(b + 4) // 8, (b + 4) % 8] = nacc_ref[i * NB : (i + 1) * NB, (j + 1) * NB : (j + 2) * NB]
        p_ref[1, 6:] = jnp.zeros_like(p_ref[1, 6:])
        for out, half in ((keep_ref, core()), (send_ref, 1 - core())):

            def put(r, _, out=out, half=half):
                rows = acc_ref[pl.ds(pl.multiple_of(half * (SK // 2) + r * 16, 16), 16), :]
                for c in range(4):
                    out[pl.ds(r * 4 + c, 1), :16, :] = rows[:, c * NB : (c + 1) * NB][None]
                block = p_ref[pl.ds(half, 1), pl.ds(r // 4, 1), pl.ds(pl.multiple_of(lax.rem(r, 4) * 32, 32), 32), :]
                out[pl.ds(r * 4, 4), 16:, :] = block.reshape(4, 8, NB)
                return 0

            lax.fori_loop(0, 32, put, 0)


def in_hbm(v):
    return pltpu.with_memory_space_constraint(v, pltpu.HBM)


def terms(matrix, targets, sign_bits, picked_rows):
    depth = 256
    whole = lambda k: (0, 0)
    return pl.pallas_call(
        terms_body,
        out_shape=[shape(UNITS, TALL, NB)] * 2,
        grid=(ROWS_DEV // depth,),
        in_specs=[
            pl.BlockSpec((depth, N), lambda k: (k, 0)),
            pl.BlockSpec((depth, NRHS), lambda k: (k, 0)),
            pl.BlockSpec((ROWS_DEV // NB, NB), whole),
            pl.BlockSpec((1, SK), whole),
        ],
        out_specs=[pl.BlockSpec((UNITS, TALL, NB), lambda k: (0, 0, 0))] * 2,
        scratch_shapes=[
            V((SK, depth), BF16),
            V((SK, NB), jnp.int32),
            V((SK, depth), BF16),
            V((SK, N), F32),
            V((N, N + NRHS), F32),
            V((2, 8, NB, NB), F32),
        ],
        compiler_params=pltpu.CompilerParams(vmem_limit_bytes=32 * MIB),
        name="terms",
    )(*map(in_hbm, (matrix, targets, sign_bits.reshape(ROWS_DEV // NB, NB), picked_rows)))


def other_core(v):
    return lax.ppermute(v, "grp", [(i, i ^ 1) for i in range(8)])


def device(g, y, z):
    return g * 32 + y * 8 + z


def over_near(v):
    groups = [
        [device(2 * x + c, y, 2 * far + near) for x in range(4) for y in range(4) for near in range(2)]
        for c in range(2)
        for far in range(4)
    ]
    return lax.all_to_all(v, ("grp", "row"), 0, 0, axis_index_groups=groups, tiled=True)


def over_far(v):
    groups = [[8 * y + 2 * far + near for far in range(4)] for y in range(4) for near in range(2)]
    return lax.all_to_all(v, "row", 0, 0, axis_index_groups=groups, tiled=True)


def summed(keep, send):
    v = (keep + other_core(send)).reshape(32, 4, TALL, NB)
    v = jnp.sum(over_near(v), axis=0)
    v = jnp.sum(over_far(jnp.broadcast_to(v, (4, 4, TALL, NB))), axis=0)
    v = over_near(jnp.broadcast_to(v, (32, 4, TALL, NB)))
    return v.reshape(UNITS, TALL, NB)


def gram_body(in_ref, out_ref, s_ref):
    def take(r, _):
        for c in range(4):
            s_ref[pl.ds(pl.multiple_of(r * 16, 16), 16), c * NB : (c + 1) * NB] = in_ref[pl.ds(r * 4 + c, 1), :16, :][0]
        out_ref[pl.ds(pl.multiple_of(len(LOWER) * NB + r * 32, 32), 32), :] = in_ref[pl.ds(r * 4, 4), 16:, :].reshape(32, NB)
        return 0

    lax.fori_loop(0, 32, take, 0)
    hi, lo = split(s_ref[...])
    hit, lot = hi.T, lo.T
    for i in range(4):
        rows, wide = slice(i * NB, (i + 1) * NB), (i + 1) * NB
        g = dot(hit[rows], hi[:, :wide]) + (dot(hit[rows], lo[:, :wide]) + dot(lot[rows], hi[:, :wide]))
        for j in range(i + 1):
            b = LOWER.index((i, j))
            out_ref[b * NB : (b + 1) * NB, :] = g[:, j * NB : (j + 1) * NB]


def gram(v):
    return pl.pallas_call(
        gram_body,
        out_shape=shape((len(LOWER) + 8) * NB, NB),
        in_specs=[pl.BlockSpec(memory_space=V)],
        out_specs=pl.BlockSpec(memory_space=V),
        scratch_shapes=[V((SK // 2, N), F32)],
        compiler_params=pltpu.CompilerParams(vmem_limit_bytes=16 * MIB),
        name="gram",
    )(v)


def rows_of(v, k):
    return jnp.broadcast_to(v[k : k + 1, :], (8, v.shape[1]))


def lanes_of(v, j):
    return jnp.broadcast_to(v[:, j : j + 1], (8, NB))


def tree(vs):
    while len(vs) > 1:
        vs = [vs[i] + vs[i + 1] for i in range(0, len(vs) - 1, 2)] + ([vs[-1]] if len(vs) % 2 else [])
    return vs[0]


def factor_block(block, u_ref, d_ref, w_ref):
    lane = lax.broadcasted_iota(jnp.int32, (8, NB), 1)
    sub = lax.broadcasted_iota(jnp.int32, (8, NB), 0)

    def packed(vs):
        v = vs[0]
        for m in range(1, 8):
            v = jnp.where(sub == m, vs[m], v)
        return v

    tiles = list(block)
    last = NB // 8 - 1
    cols = [lanes_of(tiles[0], m) for m in range(8)]
    for p in range(last + 1):
        q = 8 * p
        t = tiles[p]
        inside = (lane >= q) & (lane < q + 8)
        own = jnp.where(inside, jnp.where(lane == q + sub, 1.0, 0.0), t)
        own = [rows_of(own, m) for m in range(8)]
        close = [i for i in (p + 1, p + 2) if i <= last]
        near = {i: [lanes_of(tiles[i], q + m) for m in range(8)] for i in close}
        ahead = [lanes_of(tiles[p + 1], q + 8 + m) for m in range(8)] if close else None
        l, r, u = {}, {}, []
        c = {i: [] for i in close}
        diag = jnp.zeros((8, NB), F32)
        for m in range(8):
            pivot = rows_of(cols[m], m)
            r[m] = lax.rsqrt(pivot)
            low = cols[m] * r[m]
            diag = jnp.where(lane == q + m, low, diag)
            for k in range(m + 1, 8):
                l[k, m] = rows_of(low, k)
                cols[k] = cols[k] - low * l[k, m]
            for i in close:
                c[i].append(near[i][m] * r[m])
                for k in range(m + 1, 8):
                    near[i][k] = near[i][k] - l[k, m] * c[i][m]
            if close:
                ahead = [ahead[n] - c[p + 1][m] * rows_of(c[p + 1][m], n) for n in range(8)]
            u.append(own[m] * r[m])
            for k in range(m + 1, 8):
                own[k] = own[k] - l[k, m] * u[m]
        for i in close:
            cleared = jnp.where(inside, 0.0, tiles[i])
            tiles[i] = cleared - tree([c[i][m] * u[m] for m in range(8)])
        cols = ahead
        flat = packed(u)
        w_ref[q : q + 8, :] = jnp.where(lane < q + 8, flat, 0.0)
        u_ref[q : q + 8, :] = jnp.where(lane >= q + 8, flat, 0.0)
        d_ref[q : q + 8, :] = jnp.where(q + sub >= lane, diag, 0.0)
        if p + 3 <= last:
            z = [None] * 8
            for m in range(7, -1, -1):
                v = u[m]
                for k in range(m + 1, 8):
                    v = v - l[k, m] * z[k]
                z[m] = v * r[m]
            for i in range(p + 3, last + 1):
                v = tiles[i]
                cleared = jnp.where(inside, 0.0, v)
                tiles[i] = cleared - tree([lanes_of(v, q + m) * z[m] for m in range(8)])


def finish_body(
    gram_scale, grad_scale, own_ref, got_ref, mat_ref, t_ref, l_ref, x_ref, r_hbm,
    a_ref, b_ref, lt_ref, li_ref, m_ref, d_ref, r_ref, sems,
):
    for b, (i, j) in enumerate(LOWER):
        rows = slice(b * NB, (b + 1) * NB)
        g = (own_ref[rows, :] + got_ref[rows, :]) * gram_scale
        a_ref[j * NB : (j + 1) * NB, i * NB : (i + 1) * NB] = g.T if i != j else g
    for i, j in LOWER:
        if i != j:
            zeros = jnp.zeros((NB, NB), F32)
            lt_ref[i * NB : (i + 1) * NB, j * NB : (j + 1) * NB] = zeros
            li_ref[j * NB : (j + 1) * NB, i * NB : (i + 1) * NB] = zeros
    for j in range(N // NB):
        o, e, f = j * NB, (j + 1) * NB, (j + 2) * NB
        tiles = [a_ref[o + 8 * i : o + 8 * i + 8, o:e] for i in range(NB // 8)]
        factor_block(tiles, lt_ref.at[o:e, o:e], d_ref.at[o:e, :], li_ref.at[o:e, o:e])
        w = li_ref[o:e, o:e]
        if e < N:
            u = dot_hi(w, a_ref[o:e, e:f])
            ut = u.T
            lt_ref[o:e, e:f] = u
            a_ref[e:f, e:f] = a_ref[e:f, e:f] - dot_hi(ut, u)
        if j:
            li_ref[o:e, 0:o] = dot_parts(w, b_ref[o:e, 0:o])
        if f < N:
            rest = dot_hi(w, a_ref[o:e, f:])
            lt_ref[o:e, f:] = rest
            a_ref[e:f, f:] = a_ref[e:f, f:] - dot_hi(ut, rest)
            for g in range(f, N, NB):
                h = g + NB
                a_ref[g:h, g:] = a_ref[g:h, g:] - dot_hi(lt_ref[o:e, g:h].T, lt_ref[o:e, g:])
        for g in range(e, N, NB):
            h = g + NB
            new = dot_parts(ut if g == e else lt_ref[o:e, g:h].T, li_ref[o:e, 0:e])
            if j:
                b_ref[g:h, 0:o] = b_ref[g:h, 0:o] - new[:, :o]
            b_ref[g:h, o:e] = -new[:, o:]
    l_ref[...] = lt_ref[...].T
    for o in range(0, N, NB):
        e = o + NB
        l_ref[o:e, o:e] = lt_ref[o:e, o:e].T + d_ref[o:e, :]

    base = len(LOWER) * NB

    def moment(b):
        at = pl.ds(base + (b % 8) * NB, NB)
        mine = own_ref[at, :]
        other = got_ref[at, :]
        return jnp.where(core() == b // 8, mine, other) * grad_scale

    first = jnp.concatenate([moment(i) for i in range(4)], axis=0)
    for b, (i, j) in enumerate(LOWER):
        g = moment(b + 4)
        m_ref[i * NB : (i + 1) * NB, j * NB : (j + 1) * NB] = g
        if i != j:
            m_ref[j * NB : (j + 1) * NB, i * NB : (i + 1) * NB] = g.T

    def times(parts, v):
        hi, lo = split(v)
        both = jnp.concatenate([hi, lo], axis=1)
        ahead, behind = dot(parts[0], both), dot(parts[1], both)
        return ahead[:, :NRHS] + ((ahead[:, NRHS:] + behind[:, :NRHS]) + behind[:, NRHS:])

    inverse, turned, moments = split(li_ref[...]), split(li_ref[...].T), split(m_ref[...])
    x = times(turned, times(inverse, first))
    for _ in range(ITERS - 1):
        x = x + times(turned, times(inverse, first - times(moments, x)))
    x_ref[...] = x
    xs = jnp.concatenate(split(x), axis=1)
    puts = []
    deep = ROWS_DEV // 2
    for c in range(2):
        rows = slice(c * deep, (c + 1) * deep)
        hi, lo = split(mat_ref[rows, :])
        ahead, behind = dot(hi, xs), dot(lo, xs)
        r_ref[rows, :] = t_ref[rows, :] - (ahead[:, :NRHS] + ((ahead[:, NRHS:] + behind[:, :NRHS]) + behind[:, NRHS:]))
        puts.append(pltpu.make_async_copy(r_ref.at[rows, :], r_hbm.at[rows, :], sems.at[c]))
        puts[-1].start()
    for copy in puts:
        copy.wait()


def finished(own, got, matrix, targets, gram_scale, grad_scale):
    def body(*refs):
        finish_body(gram_scale, grad_scale, *refs)

    vmem, hbm = pl.BlockSpec(memory_space=V), pl.BlockSpec(memory_space=pl.ANY)
    return pl.pallas_call(
        body,
        out_shape=[shape(N, N), shape(N, NRHS), shape(ROWS_DEV, NRHS)],
        in_specs=[vmem] * 4,
        out_specs=[vmem, vmem, hbm],
        scratch_shapes=[V((N, N), F32)] * 5 + [V((N, NB), F32), V((ROWS_DEV, NRHS), F32), pltpu.SemaphoreType.DMA((2,))],
        compiler_params=pltpu.CompilerParams(vmem_limit_bytes=32 * MIB),
        name="finish",
    )(own, got, matrix, targets)


def on_device(matrix, targets, sign_bits, picked_rows):
    total_rows = matrix.shape[0] * lax.axis_size("grp") * lax.axis_size("row")
    keep, send = terms(matrix, targets, sign_bits, picked_rows)
    own = gram(summed(keep, send))
    return tuple(finished(own, other_core(own), matrix, targets, N / (SK * total_rows), N / total_rows))


def solution(mesh):
    rows = P(("grp", "row"), None)
    return jax.shard_map(
        on_device,
        mesh=mesh,
        in_specs=(rows, rows, P(("grp", "row")), rows),
        out_specs=(P(), P(), rows),
        check_vma=False,
    )
```
